32 devices in a mesh: parts: 2 (over y), shard: 4 (over z), layer: 2 (over x), sub: 2 (over core).
Axes of the slice: x: 2, y: 2, z: 4, core: 2. Of those that a mesh axis runs over, the one named last changes fastest.
Arguments:
- act_in: bfloat16 [2, 1024, 14336], P('layer', ('parts', 'shard'), 'sub'), parts along dimension 1, may hold values from -6 to 6
- grad_out: bfloat16 [2, 1024, 8192], P('layer', ('parts', 'shard'), 'sub'), parts along dimension 1, may hold values from -6 to 6
- factor_in: bfloat16 [2, 12, 32, 14336], P('layer', 'shard', None, 'sub'), may hold values from -0.046875 to 0.046875
- factor_out: bfloat16 [2, 12, 32, 8192], P('layer', 'shard', None, 'sub'), may hold values from -0.0625 to 0.0625
- query_row: int32 [12], replicated, may hold values from 0 to 11, as said below
- pairs: int32 [2, 4, 12], replicated, may hold values from 0 to 1, as said below
Outputs:
- scores: float32 [1024, 12], P(('parts', 'shard'), 'layer'), parts along dimension 0
The draws below stay inside these ranges and needn't reach their ends.
There are 2 independent parts, one for each index of `parts`. The reference program is written for one: setup_inputs(seed, part) draws one part's arguments, and reference() takes and returns one part's arrays. A program takes and returns all parts, laid end to end along the dimension named above; an argument that names none is the same for every part. Nothing has to cross between parts.
Inputs may be any that keep to these rules, and one draw needn't show every extreme that they name: A permutation: query q's factors are row query_row[q] of factor_in and factor_out. `pairs`: for each layer, shard and k, at most one listed query has its stored row in k * 3 to (k + 1) * 3 - 1; in every layer some shard lists one query for every k.
All inputs are finite; a program needn't handle non-finite values.
Results may differ from the reference program's by a relative error of at most 0.0003.
Values may be sent and summed in bfloat16 or wider, within the bound.
No kernel may reach another device: no remote copies, remote signals or barrier semaphores. Data moves between devices by JAX's collectives and lax.ppermute only.
A program may use at most 64 MiB of HBM per device.

```python
import jax
import jax.numpy as jnp
from jax import lax

D = 8192
FF = 14336
R = 32
Q_DEV = 3
TOK_DEV = 128
LAYERS = 2
TOKENS = 512
QUERIES = 12
N_SHARD = 4


def routing_tables(key):
    query_row = jax.random.permutation(jax.random.fold_in(key, 11), QUERIES).astype(jnp.int32)
    pick_local = jax.random.randint(jax.random.fold_in(key, 12), (LAYERS, N_SHARD, N_SHARD), 0, Q_DEV)
    level = jax.random.randint(jax.random.fold_in(key, 13), (LAYERS, N_SHARD), 2, N_SHARD + 1)
    full_shard = jax.random.randint(jax.random.fold_in(key, 14), (LAYERS,), 0, N_SHARD)
    shard_ids = jnp.arange(N_SHARD, dtype=jnp.int32)
    level = jnp.where(shard_ids[None, :] == full_shard[:, None], N_SHARD, level)
    coin = jax.random.randint(jax.random.fold_in(key, 15), (LAYERS, N_SHARD, N_SHARD), 0, N_SHARD)
    live_pick = coin < level[:, :, None]
    owner_of = query_row // Q_DEV
    local_of = query_row % Q_DEV
    live_query = live_pick[:, :, owner_of]
    match_query = pick_local[:, :, owner_of] == local_of[None, None, :]
    pairs = jnp.logical_and(live_query, match_query).astype(jnp.int32)
    return (query_row, pairs)


def draw_query_row(key, part):
    return routing_tables(key)[0]


def draw_pairs(key, part):
    return routing_tables(key)[1]


def block_scale(own_key, shape, shards, least, top_value):
    loudness, own = 1.0, jax.random.fold_in(own_key, 6)
    for dim, parts in shards:
        heights = jnp.exp(jax.random.uniform(jax.random.fold_in(own, dim), (parts,), jnp.float32, least / len(shards), top_value / len(shards)))
        loudness = loudness * jnp.repeat(heights, shape[dim] // parts).reshape([-1 if axis == dim else 1 for axis in range(len(shape))])
    return loudness


def centred(key, extent, deviation, bound, shards=(), held_as=jnp.bfloat16):
    result = deviation * jax.random.normal(key, extent, jnp.float32)
    if shards:
        result = result * block_scale(key, extent, shards, -0.22, 0.18)
    return jnp.clip(result, -bound, bound).astype(held_as)


def setup_inputs(seed: int = 0, part: int = 0) -> dict:
    seeds = jax.random.split(jax.random.key(seed), 7)
    part_splits = jax.random.split(jax.random.fold_in(seeds[6], part), 7)
    return {
        "act_in": centred(part_splits[0], (LAYERS, TOKENS, FF), 1.0, 6.0, ((0, 2), (1, 4), (2, 2))),
        "grad_out": centred(part_splits[1], (LAYERS, TOKENS, D), 1.0, 6.0, ((0, 2), (1, 4), (2, 2))),
        "factor_in": centred(seeds[2], (LAYERS, QUERIES, R, FF), FF ** -0.5, 0.046875, ((0, 2), (1, 4), (3, 2))),
        "factor_out": centred(seeds[3], (LAYERS, QUERIES, R, D), D ** -0.5, 0.0625, ((0, 2), (1, 4), (3, 2))),
        "query_row": draw_query_row(jax.random.fold_in(seeds[6], 71), part),
        "pairs": draw_pairs(jax.random.fold_in(seeds[6], 71), part),
    }


def reference(act_in, grad_out, factor_in, factor_out, query_row, pairs):
    owner_of = query_row // Q_DEV
    shard_ids = jnp.arange(N_SHARD, dtype=jnp.int32)
    owner_onehot = (owner_of[None, :] == shard_ids[:, None]).astype(jnp.int32)

    def score_block(block_index):
        which_layer = (block_index // N_SHARD).astype(jnp.int32)
        shard_pos = (block_index % N_SHARD).astype(jnp.int32)
        listed = pairs[which_layer, shard_pos]
        chosen = owner_onehot * listed[None, :]
        live_slot = jnp.sum(chosen, axis=1)
        pick_row = jnp.sum(chosen * query_row[None, :], axis=1).astype(jnp.int32)
        pick_row = jnp.where(live_slot > 0, pick_row, shard_ids * Q_DEV).astype(jnp.int32)
        out_factor = factor_out[which_layer][pick_row].reshape(N_SHARD * R, D)
        in_factor = factor_in[which_layer][pick_row].reshape(N_SHARD * R, FF)
        start = (shard_pos * TOK_DEV).astype(jnp.int32)
        grad_rows = lax.dynamic_slice_in_dim(grad_out[which_layer], start, TOK_DEV, 0)
        act_rows = lax.dynamic_slice_in_dim(act_in[which_layer], start, TOK_DEV, 0)
        proj_out = jnp.dot(grad_rows, out_factor.T, preferred_element_type=jnp.float32)
        proj_in = jnp.dot(act_rows, in_factor.T, preferred_element_type=jnp.float32)
        slot_score = jnp.sum((proj_out * proj_in).reshape(TOK_DEV, N_SHARD, R), axis=2)
        return jnp.dot(slot_score, chosen.astype(jnp.float32), precision=lax.Precision.HIGHEST)

    blocks = lax.map(score_block, jnp.arange(LAYERS * N_SHARD, dtype=jnp.int32))
    blocks = blocks.reshape(LAYERS, N_SHARD, TOK_DEV, QUERIES)
    return jnp.sum(blocks, axis=0).reshape(TOKENS, QUERIES)
```

```python
import itertools

import jax
import jax.numpy as jnp
from jax import lax
from jax.sharding import PartitionSpec as P


def offsets(axes):
    sizes = [lax.axis_size(a) for a in axes]
    places = list(itertools.product(*[range(n) for n in sizes]))
    for shift in places[1:]:
        pairs = []
        for i, place in enumerate(places):
            moved = tuple((a + b) % n for a, b, n in zip(place, shift, sizes))
            pairs.append((i, places.index(moved)))
        yield shift, pairs


def shards(act_in, grad_out, factor_in, factor_out, query_row, pairs):
    parts = lax.axis_size("parts")
    shard_count = lax.axis_size("shard")
    layers = lax.axis_size("layer")
    subs = lax.axis_size("sub")
    my_part = lax.axis_index("parts")
    my_shard = lax.axis_index("shard")
    my_layer = lax.axis_index("layer")
    my_sub = lax.axis_index("sub")
    per_owner, rank = factor_out.shape[1], factor_out.shape[2]
    tokens = act_in.shape[1]
    wide_out = grad_out.shape[2] // parts
    wide_in = act_in.shape[2] // parts
    queries = query_row.shape[0]

    layer_pairs = lax.dynamic_index_in_dim(pairs, my_layer, 0, keepdims=False)
    owner_of = query_row // per_owner
    mine = (owner_of == my_shard).astype(jnp.int32)
    local_row = jnp.sum(layer_pairs * (mine * (query_row % per_owner))[None, :], axis=1)

    def factor_part(dest, part):
        row = lax.dynamic_index_in_dim(local_row, dest, 0, keepdims=False)
        piece_out = lax.dynamic_slice(factor_out, (0, row, 0, part * wide_out), (1, 1, rank, wide_out))
        piece_in = lax.dynamic_slice(factor_in, (0, row, 0, part * wide_in), (1, 1, rank, wide_in))
        return jnp.concatenate([piece_out[0, 0], piece_in[0, 0]], axis=1)

    def token_part(part):
        piece_out = lax.dynamic_slice(grad_out, (0, 0, part * wide_out), (1, tokens, wide_out))
        piece_in = lax.dynamic_slice(act_in, (0, 0, part * wide_in), (1, tokens, wide_in))
        return jnp.concatenate([piece_out[0], piece_in[0]], axis=1)

    slots = [factor_part(my_shard, my_part)]
    for d in range(1, shard_count):
        shift = [(i, (i + d) % shard_count) for i in range(shard_count)]
        sent = factor_part((my_shard + d) % shard_count, my_part)
        slots.append(lax.ppermute(sent, "shard", shift))
    rows = [token_part(my_part)]
    for e in range(1, parts):
        shift = [(i, (i + e) % parts) for i in range(parts)]
        rows.append(lax.ppermute(token_part((my_part + e) % parts), "parts", shift))

    factors = jnp.concatenate(slots, axis=0)
    dims = (((1,), (1,)), ((), ()))
    proj = [
        jnp.stack([
            lax.dot_general(factors[:, :wide_out], x[:, :wide_out], dims, preferred_element_type=jnp.float32),
            lax.dot_general(factors[:, wide_out:], x[:, wide_out:], dims, preferred_element_type=jnp.float32),
        ]).reshape(2, shard_count, rank, tokens)
        for x in rows
    ]
    half = rank // subs

    def piece(e, sub):
        return lax.dynamic_slice_in_dim(proj[e], sub * half, half, 2)

    total = piece(0, my_sub)
    for (e, f), shift in offsets(("parts", "sub")):
        sent = piece((parts - e) % parts, (my_sub + f) % subs)
        total = total + lax.ppermute(sent, ("parts", "sub"), shift)
    slot_score = jnp.sum(total[0] * total[1], axis=1)

    owners = (my_shard - jnp.arange(shard_count, dtype=jnp.int32)) % shard_count
    listed = lax.dynamic_index_in_dim(layer_pairs, my_shard, 0, keepdims=False)
    columns = ((owner_of[:, None] == owners[None, :]).astype(jnp.int32) * listed[:, None]).astype(jnp.float32)
    part_scores = jnp.dot(columns, slot_score, precision=lax.Precision.HIGHEST)

    wide = queries // layers

    def block(layer):
        return lax.dynamic_slice_in_dim(part_scores, layer * wide, wide, 0)

    layer_sums = [block(my_layer)] + [None] * (layers - 1)
    for (e, f), shift in offsets(("layer", "sub")):
        got = lax.ppermute(block((my_layer + e) % layers), ("layer", "sub"), shift)
        layer_sums[e] = got if layer_sums[e] is None else layer_sums[e] + got
    out = sum(layer_sums[1:], layer_sums[0])
    return out.T


def solution(mesh):
    in_specs = (
        P("layer", ("parts", "shard"), "sub"),
        P("layer", ("parts", "shard"), "sub"),
        P("layer", "shard", None, "sub"),
        P("layer", "shard", None, "sub"),
        P(),
        P(),
    )
    out_specs = P(("parts", "shard"), "layer")
    return jax.shard_map(shards, mesh=mesh, in_specs=in_specs, out_specs=out_specs, check_vma=False)
```

```python
import functools
import itertools

import jax
import jax.numpy as jnp
from jax import lax
from jax.experimental import pallas as pl
from jax.experimental.pallas import tpu as pltpu
from jax.sharding import PartitionSpec as P


def offsets(axes):
    sizes = [lax.axis_size(a) for a in axes]
    places = list(itertools.product(*[range(n) for n in sizes]))
    for shift in places[1:]:
        pairs = []
        for i, place in enumerate(places):
            moved = tuple((a + b) % n for a, b, n in zip(place, shift, sizes))
            pairs.append((i, places.index(moved)))
        yield shift, pairs


def wrap(i, n):
    return jnp.where(i >= n, i - n, i)


def pick_rows(query_row, pairs, per_owner, dests):
    base = lax.axis_index("shard") * per_owner
    layer = lax.axis_index("layer")

    def step(q, rows):
        row = query_row[q] - base
        held = jnp.logical_and(row >= 0, row < per_owner)
        row = jnp.where(held, row, 0)
        return tuple(r + pairs[layer, dest, q] * row for r, dest in zip(rows, dests))

    count = query_row.shape[0]
    rows = lax.fori_loop(0, count, step, (jnp.int32(0),) * len(dests), unroll=count <= 16)
    return [jnp.clip(row, 0, per_owner - 1) for row in rows]


def send_kernel(parts, shard_count, query_row, pairs, act, grad, factor_in, factor_out, *refs):
    sent, sem = refs[:-1], refs[-1]
    my_part, my_shard = lax.axis_index("parts"), lax.axis_index("shard")
    wide_out, wide_in = grad.shape[2] // parts, act.shape[2] // parts
    copies = []

    def span(part, wide):
        return pl.ds(pl.multiple_of(part * wide, 128), wide)

    def start(source_out, source_in, target):
        for source, place in ((source_out, pl.ds(0, wide_out)), (source_in, pl.ds(wide_out, wide_in))):
            copies.append(pltpu.make_async_copy(source, target.at[:, place], sem.at[len(copies)]))
            copies[-1].start()

    for e in range(1, parts):
        part = wrap(my_part + e, parts)
        start(grad.at[0, :, span(part, wide_out)], act.at[0, :, span(part, wide_in)], sent[shard_count - 1 + e - 1])
    dests = [wrap(my_shard + d, shard_count) for d in range(1, shard_count)]
    for d, row in enumerate(pick_rows(query_row, pairs, factor_out.shape[1], dests)):
        start(factor_out.at[0, row, :, span(my_part, wide_out)], factor_in.at[0, row, :, span(my_part, wide_in)], sent[d])
    for copy in copies:
        copy.wait()


def make_sends(act, grad, factor_in, factor_out, query_row, pairs):
    parts, shard_count = lax.axis_size("parts"), lax.axis_size("shard")
    rank, tokens = factor_out.shape[2], act.shape[1]
    wide = (grad.shape[2] + act.shape[2]) // parts
    shapes = [jax.ShapeDtypeStruct((rank, wide), act.dtype)] * (shard_count - 1)
    shapes += [jax.ShapeDtypeStruct((tokens, wide), act.dtype)] * (parts - 1)
    smem, in_hbm = pl.BlockSpec(memory_space=pltpu.SMEM), pl.BlockSpec(memory_space=pltpu.HBM)
    sent = pl.pallas_call(
        functools.partial(send_kernel, parts, shard_count),
        out_shape=shapes,
        in_specs=[smem, smem] + [in_hbm] * 4,
        out_specs=[pl.BlockSpec(memory_space=pltpu.VMEM)] * len(shapes),
        scratch_shapes=[pltpu.SemaphoreType.DMA((2 * len(shapes),))],
        compiler_params=pltpu.CompilerParams(vmem_limit_bytes=60 * 2**20),
        name="make_sends",
    )(query_row, pairs, act, grad, factor_in, factor_out)
    return sent[: shard_count - 1], sent[shard_count - 1 :]


def own_kernel(parts, query_row, pairs, act, grad, factor_in, factor_out, rows, slot, sem):
    my_part = lax.axis_index("parts")
    wide_out, wide_in = grad.shape[2] // parts, act.shape[2] // parts
    span_out = pl.ds(pl.multiple_of(my_part * wide_out, 128), wide_out)
    span_in = pl.ds(pl.multiple_of(my_part * wide_in, 128), wide_in)
    to_out, to_in = pl.ds(0, wide_out), pl.ds(wide_out, wide_in)
    (row,) = pick_rows(query_row, pairs, factor_out.shape[1], [lax.axis_index("shard")])
    copies = [
        pltpu.make_async_copy(grad.at[0, :, span_out], rows.at[:, to_out], sem.at[0]),
        pltpu.make_async_copy(act.at[0, :, span_in], rows.at[:, to_in], sem.at[1]),
        pltpu.make_async_copy(factor_out.at[0, row, :, span_out], slot.at[:, to_out], sem.at[2]),
        pltpu.make_async_copy(factor_in.at[0, row, :, span_in], slot.at[:, to_in], sem.at[3]),
    ]
    for copy in copies:
        copy.start()
    for copy in copies:
        copy.wait()


def make_own(act, grad, factor_in, factor_out, query_row, pairs):
    parts = lax.axis_size("parts")
    rank, tokens = factor_out.shape[2], act.shape[1]
    wide = (grad.shape[2] + act.shape[2]) // parts
    smem, in_hbm = pl.BlockSpec(memory_space=pltpu.SMEM), pl.BlockSpec(memory_space=pltpu.HBM)
    return pl.pallas_call(
        functools.partial(own_kernel, parts),
        out_shape=[jax.ShapeDtypeStruct((tokens, wide), act.dtype), jax.ShapeDtypeStruct((rank, wide), act.dtype)],
        in_specs=[smem, smem] + [in_hbm] * 4,
        out_specs=[pl.BlockSpec(memory_space=pltpu.VMEM)] * 2,
        scratch_shapes=[pltpu.SemaphoreType.DMA((4,))],
        compiler_params=pltpu.CompilerParams(vmem_limit_bytes=59 * 2**20),
        name="make_own",
    )(query_row, pairs, act, grad, factor_in, factor_out)


def project_kernel(wide_out, slot, rows, out):
    dims = (((1,), (1,)), ((), ()))
    out[0] = lax.dot_general(slot[:, :wide_out], rows[:, :wide_out], dims, preferred_element_type=jnp.float32)
    out[1] = lax.dot_general(slot[:, wide_out:], rows[:, wide_out:], dims, preferred_element_type=jnp.float32)


def project(slot, rows, wide_out):
    vmem = pl.BlockSpec(memory_space=pltpu.VMEM)
    (rank, wide), tokens = slot.shape, rows.shape[0]
    return pl.pallas_call(
        functools.partial(project_kernel, wide_out),
        out_shape=jax.ShapeDtypeStruct((2, rank, tokens), jnp.float32),
        in_specs=[vmem, vmem],
        out_specs=vmem,
        compiler_params=pltpu.CompilerParams(vmem_limit_bytes=16 * 2**20),
        cost_estimate=pl.CostEstimate(flops=2 * rank * tokens * wide, bytes_accessed=2 * wide * (rank + tokens), transcendentals=0),
        name="project",
    )(slot, rows)


def shards(act_in, grad_out, factor_in, factor_out, query_row, pairs):
    parts = lax.axis_size("parts")
    shard_count = lax.axis_size("shard")
    layers = lax.axis_size("layer")
    subs = lax.axis_size("sub")
    my_shard = lax.axis_index("shard")
    my_layer = lax.axis_index("layer")
    my_sub = lax.axis_index("sub")
    per_owner, rank = factor_out.shape[1], factor_out.shape[2]
    wide_out = grad_out.shape[2] // parts
    queries = query_row.shape[0]

    args = (act_in, grad_out, factor_in, factor_out, query_row, pairs)
    sent_slots, sent_rows = make_sends(*args)
    rows = []
    for e in range(1, parts):
        shift = [(i, (i + e) % parts) for i in range(parts)]
        rows.append(lax.ppermute(sent_rows[e - 1], "parts", shift))
    slots = []
    for d in range(1, shard_count):
        shift = [(i, (i + d) % shard_count) for i in range(shard_count)]
        slots.append(lax.ppermute(sent_slots[d - 1], "shard", shift))
    own_rows, own_slot = make_own(*args)
    rows, slots = [own_rows] + rows, [own_slot] + slots

    proj = [jnp.stack([project(slot, x, wide_out) for slot in slots], axis=1) for x in rows]
    half = rank // subs

    def piece(e, sub):
        return lax.dynamic_slice_in_dim(proj[e], sub * half, half, 2)

    total = piece(0, my_sub)
    for (e, f), shift in offsets(("parts", "sub")):
        sent = piece((parts - e) % parts, (my_sub + f) % subs)
        total = total + lax.ppermute(sent, ("parts", "sub"), shift)
    slot_score = jnp.sum(total[0] * total[1], axis=1)

    owner_of = query_row // per_owner
    layer_pairs = lax.dynamic_index_in_dim(pairs, my_layer, 0, keepdims=False)
    owners = (my_shard - jnp.arange(shard_count, dtype=jnp.int32)) % shard_count
    listed = lax.dynamic_index_in_dim(layer_pairs, my_shard, 0, keepdims=False)
    columns = ((owner_of[:, None] == owners[None, :]).astype(jnp.int32) * listed[:, None]).astype(jnp.float32)
    part_scores = jnp.dot(columns, slot_score, precision=lax.Precision.HIGHEST)

    wide = queries // layers

    def block(layer):
        return lax.dynamic_slice_in_dim(part_scores, layer * wide, wide, 0)

    layer_sums = [block(my_layer)] + [None] * (layers - 1)
    for (e, f), shift in offsets(("layer", "sub")):
        got = lax.ppermute(block((my_layer + e) % layers), ("layer", "sub"), shift)
        layer_sums[e] = got if layer_sums[e] is None else layer_sums[e] + got
    out = sum(layer_sums[1:], layer_sums[0])
    return out.T


def solution(mesh):
    in_specs = (
        P("layer", ("parts", "shard"), "sub"),
        P("layer", ("parts", "shard"), "sub"),
        P("layer", "shard", None, "sub"),
        P("layer", "shard", None, "sub"),
        P(),
        P(),
    )
    out_specs = P(("parts", "shard"), "layer")
    return jax.shard_map(shards, mesh=mesh, in_specs=in_specs, out_specs=out_specs, check_vma=False)
```

```python
import functools
import itertools

import jax
import jax.numpy as jnp
from jax import lax
from jax.experimental import pallas as pl
from jax.experimental.pallas import tpu as pltpu
from jax.sharding import PartitionSpec as P


def offsets(axes):
    sizes = [lax.axis_size(a) for a in axes]
    places = list(itertools.product(*[range(n) for n in sizes]))
    for shift in places[1:]:
        pairs = []
        for i, place in enumerate(places):
            moved = tuple((a + b) % n for a, b, n in zip(place, shift, sizes))
            pairs.append((i, places.index(moved)))
        yield shift, pairs


def wrap(i, n):
    return jnp.where(i >= n, i - n, i)


def pick_rows(query_row, pairs, per_owner, dests):
    base = lax.axis_index("shard") * per_owner
    layer = lax.axis_index("layer")

    def step(q, rows):
        row = query_row[q] - base
        held = jnp.logical_and(row >= 0, row < per_owner)
        row = jnp.where(held, row, 0)
        return tuple(r + pairs[layer, dest, q] * row for r, dest in zip(rows, dests))

    count = query_row.shape[0]
    rows = lax.fori_loop(0, count, step, (jnp.int32(0),) * len(dests), unroll=count <= 16)
    return [jnp.clip(row, 0, per_owner - 1) for row in rows]


def start_tables(query_hbm, pairs_hbm, query_row, pairs, sem):
    copies = [pltpu.make_async_copy(query_hbm, query_row, sem.at[0]), pltpu.make_async_copy(pairs_hbm, pairs, sem.at[1])]
    for copy in copies:
        copy.start()
    return copies


def table_scratch(query_row, pairs):
    return [pltpu.SMEM(query_row.shape, query_row.dtype), pltpu.SMEM(pairs.shape, pairs.dtype)]


def send_kernel(parts, shard_count, query_hbm, pairs_hbm, act, grad, factor_in, factor_out, *refs):
    sent, (query_row, pairs, sem, table_sem) = refs[:-4], refs[-4:]
    tables = start_tables(query_hbm, pairs_hbm, query_row, pairs, table_sem)
    my_part, my_shard = lax.axis_index("parts"), lax.axis_index("shard")
    wide_out, wide_in = grad.shape[2] // parts, act.shape[2] // parts
    copies = []

    def span(part, wide):
        return pl.ds(pl.multiple_of(part * wide, 128), wide)

    def start(source_out, source_in, target):
        for source, place in ((source_out, pl.ds(0, wide_out)), (source_in, pl.ds(wide_out, wide_in))):
            copies.append(pltpu.make_async_copy(source, target.at[:, place], sem.at[len(copies)]))
            copies[-1].start()

    for e in range(1, parts):
        part = wrap(my_part + e, parts)
        start(grad.at[0, :, span(part, wide_out)], act.at[0, :, span(part, wide_in)], sent[shard_count - 1 + e - 1])
    for table in tables:
        table.wait()
    dests = [wrap(my_shard + d, shard_count) for d in range(1, shard_count)]
    for d, row in enumerate(pick_rows(query_row, pairs, factor_out.shape[1], dests)):
        start(factor_out.at[0, row, :, span(my_part, wide_out)], factor_in.at[0, row, :, span(my_part, wide_in)], sent[d])
    for copy in copies:
        copy.wait()


def make_sends(act, grad, factor_in, factor_out, query_row, pairs):
    parts, shard_count = lax.axis_size("parts"), lax.axis_size("shard")
    rank, tokens = factor_out.shape[2], act.shape[1]
    wide = (grad.shape[2] + act.shape[2]) // parts
    shapes = [pltpu.VMEM((rank, wide), act.dtype)] * (shard_count - 1)
    shapes += [pltpu.VMEM((tokens, wide), act.dtype)] * (parts - 1)
    sent = pl.pallas_call(
        functools.partial(send_kernel, parts, shard_count),
        out_shape=shapes,
        in_specs=[pl.BlockSpec(memory_space=pltpu.HBM)] * 6,
        out_specs=[pl.BlockSpec(memory_space=pltpu.VMEM)] * len(shapes),
        scratch_shapes=table_scratch(query_row, pairs) + [pltpu.SemaphoreType.DMA((2 * len(shapes),)), pltpu.SemaphoreType.DMA((2,))],
        compiler_params=pltpu.CompilerParams(vmem_limit_bytes=2**22),
        name="make_sends",
    )(query_row, pairs, act, grad, factor_in, factor_out)
    return sent[: shard_count - 1], sent[shard_count - 1 :]


def own_kernel(parts, query_hbm, pairs_hbm, act, grad, factor_in, factor_out, rows, slot, query_row, pairs, sem, table_sem):
    for table in start_tables(query_hbm, pairs_hbm, query_row, pairs, table_sem):
        table.wait()
    my_part = lax.axis_index("parts")
    wide_out, wide_in = grad.shape[2] // parts, act.shape[2] // parts
    span_out = pl.ds(pl.multiple_of(my_part * wide_out, 128), wide_out)
    span_in = pl.ds(pl.multiple_of(my_part * wide_in, 128), wide_in)
    to_out, to_in = pl.ds(0, wide_out), pl.ds(wide_out, wide_in)
    (row,) = pick_rows(query_row, pairs, factor_out.shape[1], [lax.axis_index("shard")])
    copies = [
        pltpu.make_async_copy(grad.at[0, :, span_out], rows.at[:, to_out], sem.at[0]),
        pltpu.make_async_copy(act.at[0, :, span_in], rows.at[:, to_in], sem.at[1]),
        pltpu.make_async_copy(factor_out.at[0, row, :, span_out], slot.at[:, to_out], sem.at[2]),
        pltpu.make_async_copy(factor_in.at[0, row, :, span_in], slot.at[:, to_in], sem.at[3]),
    ]
    for copy in copies:
        copy.start()
    for copy in copies:
        copy.wait()


def make_own(act, grad, factor_in, factor_out, query_row, pairs):
    parts = lax.axis_size("parts")
    rank, tokens = factor_out.shape[2], act.shape[1]
    wide = (grad.shape[2] + act.shape[2]) // parts
    return pl.pallas_call(
        functools.partial(own_kernel, parts),
        out_shape=[pltpu.VMEM((tokens, wide), act.dtype), pltpu.VMEM((rank, wide), act.dtype)],
        in_specs=[pl.BlockSpec(memory_space=pltpu.HBM)] * 6,
        out_specs=[pl.BlockSpec(memory_space=pltpu.VMEM)] * 2,
        scratch_shapes=table_scratch(query_row, pairs) + [pltpu.SemaphoreType.DMA((4,)), pltpu.SemaphoreType.DMA((2,))],
        compiler_params=pltpu.CompilerParams(vmem_limit_bytes=2**22),
        name="make_own",
    )(query_row, pairs, act, grad, factor_in, factor_out)


def project_kernel(counts, wide_out, *refs):
    slot_count, block_count, subs = counts
    slots, blocks, outs = refs[:slot_count], refs[slot_count : slot_count + block_count], refs[slot_count + block_count :]
    my_sub = lax.axis_index("sub")
    dims = (((1,), (1,)), ((), ()))
    rank = slots[0].shape[0]
    half = rank // subs
    wide = slots[0].shape[1]
    for which, (low, high) in enumerate(((0, wide_out), (wide_out, wide))):
        left = jnp.concatenate([slot[:, low:high] for slot in slots], axis=0)
        for e, block in enumerate(blocks):
            proj = lax.dot_general(left, block[:, low:high], dims, preferred_element_type=jnp.float32)
            for j in range(slot_count):
                cuts = [proj[j * rank + c * half : j * rank + (c + 1) * half] for c in range(subs)]
                for f in range(subs):
                    sub = wrap(my_sub + f, subs)
                    cut = cuts[0]
                    for c in range(1, subs):
                        cut = jnp.where(sub == c, cuts[c], cut)
                    outs[e * subs + f][which, j] = cut


def project(slots, blocks, wide_out):
    subs = lax.axis_size("sub")
    vmem = pl.BlockSpec(memory_space=pltpu.VMEM)
    (rank, wide), tokens = slots[0].shape, blocks[0].shape[0]
    count = len(blocks) * subs
    inputs = [pltpu.with_memory_space_constraint(x, pltpu.VMEM) for x in (*slots, *blocks)]
    flops = 2 * len(slots) * rank * len(blocks) * tokens * wide
    read = 2 * wide * (len(slots) * rank + len(blocks) * tokens)
    return pl.pallas_call(
        functools.partial(project_kernel, (len(slots), len(blocks), subs), wide_out),
        out_shape=[pltpu.VMEM((2, len(slots), rank // subs, tokens), jnp.float32)] * count,
        in_specs=[vmem] * len(inputs),
        out_specs=[vmem] * count,
        compiler_params=pltpu.CompilerParams(vmem_limit_bytes=2**23),
        cost_estimate=pl.CostEstimate(flops=flops, bytes_accessed=read, transcendentals=0),
        name="project",
    )(*inputs)


def score_kernel(owners, wide, per_owner, query_hbm, pairs_hbm, *refs):
    pieces, (query_row, pairs, table_sem) = refs[:-3], refs[-3:]
    layers = lax.axis_size("layer")
    pieces, outs = pieces[:-layers], pieces[-layers:]
    tables = start_tables(query_hbm, pairs_hbm, query_row, pairs, table_sem)
    my_layer, my_shard, shard_count = lax.axis_index("layer"), lax.axis_index("shard"), lax.axis_size("shard")
    scores = []
    groups = len(owners)
    for g in range(groups):
        total = pieces[g][...]
        for piece in pieces[g + groups :: groups]:
            total = total + piece[...]
        for j in range(len(owners[g])):
            scores.append(jnp.sum(total[0, j] * total[1, j], axis=0, keepdims=True))
    slots = [d for group in owners for d in group]
    for table in tables:
        table.wait()
    for e, out in enumerate(outs):
        layer = wrap(my_layer + e, layers)
        for i in range(wide):
            q = layer * wide + i
            row = query_row[q]
            listed = pairs[my_layer, my_shard, q]
            score = jnp.zeros_like(scores[0])
            for d, slot in zip(slots, scores):
                low = wrap(my_shard + (shard_count - d) % shard_count, shard_count) * per_owner
                here = jnp.logical_and(row >= low, row < low + per_owner)
                score = score + jnp.where(here, listed, 0).astype(jnp.float32) * slot
            out[i : i + 1, :] = score


def make_scores(pieces, owners, query_row, pairs, per_owner):
    layers, tokens = lax.axis_size("layer"), pieces[0].shape[-1]
    wide = query_row.shape[0] // layers
    vmem, in_hbm = pl.BlockSpec(memory_space=pltpu.VMEM), pl.BlockSpec(memory_space=pltpu.HBM)
    pieces = [pltpu.with_memory_space_constraint(x, pltpu.VMEM) for x in pieces]
    return pl.pallas_call(
        functools.partial(score_kernel, owners, wide, per_owner),
        out_shape=[pltpu.VMEM((wide, tokens), jnp.float32)] * layers,
        in_specs=[in_hbm] * 2 + [vmem] * len(pieces),
        out_specs=[vmem] * layers,
        scratch_shapes=table_scratch(query_row, pairs) + [pltpu.SemaphoreType.DMA((2,))],
        compiler_params=pltpu.CompilerParams(vmem_limit_bytes=2**23),
        name="make_scores",
    )(query_row, pairs, *pieces)


def shards(act_in, grad_out, factor_in, factor_out, query_row, pairs):
    parts = lax.axis_size("parts")
    shard_count = lax.axis_size("shard")
    layers = lax.axis_size("layer")
    subs = lax.axis_size("sub")
    per_owner = factor_out.shape[1]
    wide_out = grad_out.shape[2] // parts

    args = [
        pltpu.with_memory_space_constraint(x, pltpu.HBM)
        for x in (act_in, grad_out, factor_in, factor_out, query_row, pairs)
    ]
    sent_slots, sent_rows = make_sends(*args)
    rows = []
    for e in range(1, parts):
        shift = [(i, (i + e) % parts) for i in range(parts)]
        rows.append(lax.ppermute(sent_rows[e - 1], "parts", shift))
    slots = []
    for d in range(1, shard_count):
        shift = [(i, (i + d) % shard_count) for i in range(shard_count)]
        slots.append(lax.ppermute(sent_slots[d - 1], "shard", shift))
    own_rows, own_slot = make_own(*args)
    rows, slots = [own_rows] + rows, [own_slot] + slots

    early, late = [0] + list(range(shard_count - 1, 2, -1)), list(range(min(2, shard_count - 1), 0, -1))
    early_own = project([slots[j] for j in early], rows[:1], wide_out)
    early_rest = project([slots[j] for j in early], rows[1:], wide_out)
    late_all = project([slots[j] for j in late], rows, wide_out)
    groups = [early_own + early_rest, late_all]
    pieces = [cuts[0] for cuts in groups]
    for (e, f), shift in offsets(("parts", "sub")):
        pieces += [lax.ppermute(cuts[(parts - e) % parts * subs + f], ("parts", "sub"), shift) for cuts in groups]
    blocks = make_scores(pieces, (tuple(early), tuple(late)), args[4], args[5], per_owner)

    layer_sums = [blocks[0]] + [None] * (layers - 1)
    for (e, f), shift in offsets(("layer", "sub")):
        got = lax.ppermute(blocks[e], ("layer", "sub"), shift)
        layer_sums[e] = got if layer_sums[e] is None else layer_sums[e] + got
    out = sum(layer_sums[1:], layer_sums[0])
    return out.T


def solution(mesh):
    in_specs = (
        P("layer", ("parts", "shard"), "sub"),
        P("layer", ("parts", "shard"), "sub"),
        P("layer", "shard", None, "sub"),
        P("layer", "shard", None, "sub"),
        P(),
        P(),
    )
    out_specs = P(("parts", "shard"), "layer")
    return jax.shard_map(shards, mesh=mesh, in_specs=in_specs, out_specs=out_specs, check_vma=False)
```

```python
import functools

import jax
import jax.numpy as jnp
from jax import lax
from jax.experimental import pallas as pl
from jax.experimental.pallas import tpu as pltpu
from jax.sharding import PartitionSpec as P


def shifted(n, d):
    return [(i, (i + d) % n) for i in range(n)]


def wrap(i, n):
    return jnp.where(i >= n, i - n, i)


def dest(shard, j, n):
    if n & (n - 1) == 0:
        return shard ^ j
    return (shard + j) % n


def source(shard, j, n):
    if n & (n - 1) == 0:
        return shard ^ j
    return (shard + n - j) % n


def slot_groups(n):
    late = list(range(max(1, n // 2), n))
    return [j for j in range(n) if j not in late], late


def start_tables(query_hbm, pairs_hbm, query_row, pairs, sem):
    copies = [pltpu.make_async_copy(query_hbm, query_row, sem.at[0]), pltpu.make_async_copy(pairs_hbm, pairs, sem.at[1])]
    for copy in copies:
        copy.start()
    return copies


def table_scratch(query_row, pairs):
    return [pltpu.SMEM(query_row.shape, query_row.dtype), pltpu.SMEM(pairs.shape, pairs.dtype)]


def pick_rows(query_row, pairs, per_owner, dests):
    base = lax.axis_index("shard") * per_owner
    layer = lax.axis_index("layer")

    def step(q, rows):
        row = query_row[q] - base
        held = jnp.logical_and(row >= 0, row < per_owner)
        row = jnp.where(held, row, 0)
        return tuple(r + pairs[layer, to, q] * row for r, to in zip(rows, dests))

    count = query_row.shape[0]
    rows = lax.fori_loop(0, count, step, (jnp.int32(0),) * len(dests), unroll=count <= 16)
    return [jnp.clip(row, 0, per_owner - 1) for row in rows]


def span(part, wide):
    return pl.ds(pl.multiple_of(part * wide, 128), wide)


def send_kernel(parts, shard_count, query_hbm, pairs_hbm, act, grad, factor_in, factor_out, *refs):
    sent, (query_row, pairs, sem, table_sem) = refs[:-4], refs[-4:]
    tables = start_tables(query_hbm, pairs_hbm, query_row, pairs, table_sem)
    my_part, my_shard = lax.axis_index("parts"), lax.axis_index("shard")
    wide_out, wide_in = grad.shape[2] // parts, act.shape[2] // parts
    copies = []

    def start(source_out, source_in, target):
        for piece, place in ((source_out, pl.ds(0, wide_out)), (source_in, pl.ds(wide_out, wide_in))):
            copies.append(pltpu.make_async_copy(piece, target.at[:, place], sem.at[len(copies)]))
            copies[-1].start()

    for e in range(1, parts):
        part = wrap(my_part + e, parts)
        start(grad.at[0, :, span(part, wide_out)], act.at[0, :, span(part, wide_in)], sent[shard_count - 1 + e - 1])
    for table in tables:
        table.wait()
    dests = [dest(my_shard, j, shard_count) for j in range(1, shard_count)]
    for k, row in enumerate(pick_rows(query_row, pairs, factor_out.shape[1], dests)):
        start(factor_out.at[0, row, :, span(my_part, wide_out)], factor_in.at[0, row, :, span(my_part, wide_in)], sent[k])
    for copy in copies:
        copy.wait()


def make_sends(act, grad, factor_in, factor_out, query_row, pairs):
    parts, shard_count = lax.axis_size("parts"), lax.axis_size("shard")
    rank, tokens = factor_out.shape[2], act.shape[1]
    wide = (grad.shape[2] + act.shape[2]) // parts
    shapes = [pltpu.VMEM((rank, wide), act.dtype)] * (shard_count - 1)
    shapes += [pltpu.VMEM((tokens, wide), act.dtype)] * (parts - 1)
    sent = pl.pallas_call(
        functools.partial(send_kernel, parts, shard_count),
        out_shape=shapes,
        in_specs=[pl.BlockSpec(memory_space=pltpu.HBM)] * 6,
        out_specs=[pl.BlockSpec(memory_space=pltpu.VMEM)] * len(shapes),
        scratch_shapes=table_scratch(query_row, pairs)
        + [pltpu.SemaphoreType.DMA((2 * len(shapes),)), pltpu.SemaphoreType.DMA((2,))],
        compiler_params=pltpu.CompilerParams(vmem_limit_bytes=2**22),
        name="make_sends",
    )(query_row, pairs, act, grad, factor_in, factor_out)
    return sent[: shard_count - 1], sent[shard_count - 1 :]


def own_kernel(parts, order, query_hbm, pairs_hbm, act, grad, factor_in, factor_out, rows, slot, weights, *scratch):
    query_row, pairs, sem, table_sem = scratch
    tables = start_tables(query_hbm, pairs_hbm, query_row, pairs, table_sem)
    my_part, my_shard, my_layer = lax.axis_index("parts"), lax.axis_index("shard"), lax.axis_index("layer")
    layers, shard_count = lax.axis_size("layer"), lax.axis_size("shard")
    per_owner, tokens = factor_out.shape[1], rows.shape[0]
    wide_out, wide_in = grad.shape[2] // parts, act.shape[2] // parts
    span_out, span_in = span(my_part, wide_out), span(my_part, wide_in)
    to_out, to_in = pl.ds(0, wide_out), pl.ds(wide_out, wide_in)
    copies = [
        pltpu.make_async_copy(grad.at[0, :, span_out], rows.at[:, to_out], sem.at[0]),
        pltpu.make_async_copy(act.at[0, :, span_in], rows.at[:, to_in], sem.at[1]),
    ]
    for copy in copies:
        copy.start()
    for table in tables:
        table.wait()
    (row,) = pick_rows(query_row, pairs, per_owner, [my_shard])
    copies += [
        pltpu.make_async_copy(factor_out.at[0, row, :, span_out], slot.at[:, to_out], sem.at[2]),
        pltpu.make_async_copy(factor_in.at[0, row, :, span_in], slot.at[:, to_in], sem.at[3]),
    ]
    for copy in copies[2:]:
        copy.start()
    wide = query_row.shape[0] // layers
    for e in range(layers):
        layer = wrap(my_layer + e, layers)
        for i in range(wide):
            q = layer * wide + i
            listed = pairs[my_layer, my_shard, q]
            for k, j in enumerate(order):
                row = query_row[q] - source(my_shard, j, shard_count) * per_owner
                here = jnp.logical_and(row >= 0, row < per_owner)
                weight = jnp.where(here, listed, 0).astype(jnp.float32)
                weights[e, k, i : i + 1, :] = jnp.full((1, tokens), weight, jnp.float32)
    for copy in copies:
        copy.wait()


def make_own(order, act, grad, factor_in, factor_out, query_row, pairs):
    parts, layers = lax.axis_size("parts"), lax.axis_size("layer")
    rank, tokens = factor_out.shape[2], act.shape[1]
    wide = (grad.shape[2] + act.shape[2]) // parts
    shapes = [
        pltpu.VMEM((tokens, wide), act.dtype),
        pltpu.VMEM((rank, wide), act.dtype),
        pltpu.VMEM((layers, len(order), query_row.shape[0] // layers, tokens), jnp.float32),
    ]
    return pl.pallas_call(
        functools.partial(own_kernel, parts, tuple(order)),
        out_shape=shapes,
        in_specs=[pl.BlockSpec(memory_space=pltpu.HBM)] * 6,
        out_specs=[pl.BlockSpec(memory_space=pltpu.VMEM)] * len(shapes),
        scratch_shapes=table_scratch(query_row, pairs) + [pltpu.SemaphoreType.DMA((4,)), pltpu.SemaphoreType.DMA((2,))],
        compiler_params=pltpu.CompilerParams(vmem_limit_bytes=2**22),
        name="make_own",
    )(query_row, pairs, act, grad, factor_in, factor_out)


def project_kernel(slot_count, block_count, subs, wide_out, *refs):
    slots, blocks, rest = refs[:slot_count], refs[slot_count : slot_count + block_count], refs[slot_count + block_count :]
    carried, outs = rest[:-subs], rest[-subs:]
    my_sub = lax.axis_index("sub")
    dims = (((1,), (1,)), ((), ()))
    rank, wide = slots[0].shape
    half = rank // subs
    before = 0
    for k, old in enumerate(carried):
        before = old.shape[2]
        first = k // subs * old.shape[0]
        outs[k % subs][first : first + old.shape[0], :, :before] = old[...]
    for which, (low, high) in enumerate(((0, wide_out), (wide_out, wide))):
        left = jnp.concatenate([slot[:, low:high] for slot in slots], axis=0)
        for e, block in enumerate(blocks):
            proj = lax.dot_general(left, block[:, low:high], dims, preferred_element_type=jnp.float32)
            for j in range(slot_count):
                cuts = [proj[j * rank + c * half : j * rank + (c + 1) * half] for c in range(subs)]
                for f in range(subs):
                    sub = wrap(my_sub + f, subs)
                    cut = cuts[0]
                    for c in range(1, subs):
                        cut = jnp.where(sub == c, cuts[c], cut)
                    outs[f][e, which, before + j] = cut


def project(slots, blocks, wide_out, carried=()):
    subs = lax.axis_size("sub")
    vmem = pl.BlockSpec(memory_space=pltpu.VMEM)
    (rank, wide), tokens = slots[0].shape, blocks[0].shape[0]
    total = len(slots) + (carried[0].shape[2] if carried else 0)
    inputs = [pltpu.with_memory_space_constraint(x, pltpu.VMEM) for x in (*slots, *blocks, *carried)]
    flops = 2 * len(slots) * rank * len(blocks) * tokens * wide
    read = 2 * wide * (len(slots) * rank + len(blocks) * tokens)
    return pl.pallas_call(
        functools.partial(project_kernel, len(slots), len(blocks), subs, wide_out),
        out_shape=[pltpu.VMEM((len(blocks), 2, total, rank // subs, tokens), jnp.float32)] * subs,
        in_specs=[vmem] * len(inputs),
        out_specs=[vmem] * subs,
        compiler_params=pltpu.CompilerParams(vmem_limit_bytes=2**23),
        cost_estimate=pl.CostEstimate(flops=flops, bytes_accessed=read, transcendentals=0),
        name="project",
    )(*inputs)


def score_kernel(here_count, weights, *refs):
    slot_count = weights.shape[1]
    pieces, out = refs[:-1], refs[-1]
    total = pieces[0][0]
    for k, piece in enumerate(pieces[1:]):
        total = total + (piece[0] if k + 1 < here_count else piece[...])
    scores = [jnp.sum(total[0, k] * total[1, k], axis=0, keepdims=True) for k in range(slot_count)]
    for e in range(weights.shape[0]):
        block = weights[e, 0] * scores[0]
        for k in range(1, slot_count):
            block = block + weights[e, k] * scores[k]
        out[e] = block


def make_scores(weights, here, far):
    layers, _, wide, tokens = weights.shape
    vmem = pl.BlockSpec(memory_space=pltpu.VMEM)
    inputs = [pltpu.with_memory_space_constraint(x, pltpu.VMEM) for x in (weights, *here, *far)]
    return pl.pallas_call(
        functools.partial(score_kernel, len(here)),
        out_shape=pltpu.VMEM((layers, wide, tokens), jnp.float32),
        in_specs=[vmem] * len(inputs),
        out_specs=vmem,
        compiler_params=pltpu.CompilerParams(vmem_limit_bytes=2**23),
        name="make_scores",
    )(*inputs)


def shards(act_in, grad_out, factor_in, factor_out, query_row, pairs):
    parts = lax.axis_size("parts")
    shard_count = lax.axis_size("shard")
    layers = lax.axis_size("layer")
    subs = lax.axis_size("sub")
    wide_out = grad_out.shape[2] // parts
    early, late = slot_groups(shard_count)

    args = [
        pltpu.with_memory_space_constraint(x, pltpu.HBM)
        for x in (act_in, grad_out, factor_in, factor_out, query_row, pairs)
    ]
    sent_slots, sent_rows = make_sends(*args)
    rows = []
    for e in range(1, parts):
        rows.append(lax.ppermute(sent_rows[e - 1], "parts", shifted(parts, e)))
    slots = [None] * shard_count
    for j in late[::-1] + early[1:]:
        to = [(i, dest(i, j, shard_count)) for i in range(shard_count)]
        slots[j] = lax.ppermute(sent_slots[j - 1], "shard", to)
    own_rows, slots[0], weights = make_own(early + late, *args)

    early_own = project([slots[j] for j in early], [own_rows], wide_out)
    early_rest = project([slots[j] for j in early], rows, wide_out) if rows else []
    cuts = project([slots[j] for j in late], [own_rows] + rows, wide_out, list(early_own) + list(early_rest))

    got = [lax.ppermute(cuts[f], "sub", shifted(subs, f)) for f in range(1, subs)]
    far = []
    for e in range(1, parts):
        total = cuts[0][e]
        for piece in got:
            total = total + piece[e]
        far.append(lax.ppermute(total, "parts", shifted(parts, parts - e)))
    blocks = make_scores(weights, [cuts[0]] + got, far)

    if subs == 2:
        blocks = blocks + lax.ppermute(blocks, "sub", shifted(subs, 1))
    else:
        blocks = lax.psum(blocks, "sub")
    out = blocks[0]
    for e in range(1, layers):
        out = out + lax.ppermute(blocks[e], "layer", shifted(layers, e))
    return out.T


def solution(mesh):
    in_specs = (
        P("layer", ("parts", "shard"), "sub"),
        P("layer", ("parts", "shard"), "sub"),
        P("layer", "shard", None, "sub"),
        P("layer", "shard", None, "sub"),
        P(),
        P(),
    )
    out_specs = P(("parts", "shard"), "layer")

    return jax.shard_map(shards, mesh=mesh, in_specs=in_specs, out_specs=out_specs, check_vma=False)
```

```python
import functools
import itertools

import jax
import jax.numpy as jnp
from jax import lax
from jax.experimental import pallas as pl
from jax.experimental.pallas import tpu as pltpu
from jax.sharding import PartitionSpec as P


def shifted(sizes, shift):
    places = list(itertools.product(*[range(n) for n in sizes]))
    return [
        (i, places.index(tuple((a + b) % n for a, b, n in zip(place, shift, sizes)))) for i, place in enumerate(places)
    ]


def wrap(i, n):
    return jnp.where(i >= n, i - n, i)


def dest(shard, j, n):
    if n & (n - 1) == 0:
        return shard ^ j
    return (shard + j) % n


def source(shard, j, n):
    if n & (n - 1) == 0:
        return shard ^ j
    return (shard + n - j) % n


def slot_groups(n):
    late = list(range(max(1, n // 2), n))
    return [j for j in range(n) if j not in late], late


def start_tables(query_hbm, pairs_hbm, query_row, pairs, sem):
    copies = [pltpu.make_async_copy(query_hbm, query_row, sem.at[0]), pltpu.make_async_copy(pairs_hbm, pairs, sem.at[1])]
    for copy in copies:
        copy.start()
    return copies


def table_scratch(query_row, pairs):
    return [pltpu.SMEM(query_row.shape, query_row.dtype), pltpu.SMEM(pairs.shape, pairs.dtype)]


def pick_rows(query_row, pairs, per_owner, dests):
    base = lax.axis_index("shard") * per_owner
    layer = lax.axis_index("layer")

    def step(q, rows):
        row = query_row[q] - base
        held = jnp.logical_and(row >= 0, row < per_owner)
        row = jnp.where(held, row, 0)
        return tuple(r + pairs[layer, to, q] * row for r, to in zip(rows, dests))

    count = query_row.shape[0]
    rows = lax.fori_loop(0, count, step, (jnp.int32(0),) * len(dests), unroll=count <= 16)
    return [jnp.clip(row, 0, per_owner - 1) for row in rows]


def span(part, wide):
    return pl.ds(pl.multiple_of(part * wide, 128), wide)


def send_kernel(parts, shard_count, query_hbm, pairs_hbm, act, grad, factor_in, factor_out, *refs):
    sent, (query_row, pairs, stored, sem, table_sem) = refs[:-5], refs[-5:]
    tables = start_tables(query_hbm, pairs_hbm, query_row, pairs, table_sem)
    my_part, my_shard = lax.axis_index("parts"), lax.axis_index("shard")
    wide_out, wide_in = grad.shape[2] // parts, act.shape[2] // parts
    to_out, to_in = pl.ds(0, wide_out), pl.ds(wide_out, wide_in)
    copies = []

    def start(piece, target):
        copies.append(pltpu.make_async_copy(piece, target, sem.at[len(copies)]))
        copies[-1].start()

    start(factor_out.at[0, :, :, span(my_part, wide_out)], stored.at[:, :, to_out])
    start(factor_in.at[0, :, :, span(my_part, wide_in)], stored.at[:, :, to_in])
    for e in range(1, parts):
        part = wrap(my_part + e, parts)
        start(grad.at[0, :, span(part, wide_out)], sent[shard_count - 1 + e - 1].at[:, to_out])
        start(act.at[0, :, span(part, wide_in)], sent[shard_count - 1 + e - 1].at[:, to_in])
    for table in tables:
        table.wait()
    dests = [dest(my_shard, j, shard_count) for j in range(1, shard_count)]
    listed = pick_rows(query_row, pairs, factor_out.shape[1], dests)
    for copy in copies[:2]:
        copy.wait()
    for target, row in zip(sent, listed):
        target[...] = stored[row]
    for copy in copies[2:]:
        copy.wait()


def make_sends(act, grad, factor_in, factor_out, query_row, pairs):
    parts, shard_count = lax.axis_size("parts"), lax.axis_size("shard")
    rank, tokens = factor_out.shape[2], act.shape[1]
    wide = (grad.shape[2] + act.shape[2]) // parts
    shapes = [pltpu.VMEM((rank, wide), act.dtype)] * (shard_count - 1)
    shapes += [pltpu.VMEM((tokens, wide), act.dtype)] * (parts - 1)
    sent = pl.pallas_call(
        functools.partial(send_kernel, parts, shard_count),
        out_shape=shapes,
        in_specs=[pl.BlockSpec(memory_space=pltpu.HBM)] * 6,
        out_specs=[pl.BlockSpec(memory_space=pltpu.VMEM)] * len(shapes),
        scratch_shapes=table_scratch(query_row, pairs)
        + [
            pltpu.VMEM((factor_out.shape[1], rank, wide), act.dtype),
            pltpu.SemaphoreType.DMA((2 * parts,)),
            pltpu.SemaphoreType.DMA((2,)),
        ],
        compiler_params=pltpu.CompilerParams(vmem_limit_bytes=2**23),
        name="make_sends",
    )(query_row, pairs, act, grad, factor_in, factor_out)
    return sent[: shard_count - 1], sent[shard_count - 1 :]


def own_kernel(parts, order, query_hbm, pairs_hbm, act, grad, factor_in, factor_out, rows, slot, weights, *scratch):
    query_row, pairs, sem, table_sem = scratch
    tables = start_tables(query_hbm, pairs_hbm, query_row, pairs, table_sem)
    my_part, my_shard, my_layer = lax.axis_index("parts"), lax.axis_index("shard"), lax.axis_index("layer")
    layers, shard_count = lax.axis_size("layer"), lax.axis_size("shard")
    per_owner, tokens = factor_out.shape[1], rows.shape[0]
    wide_out, wide_in = grad.shape[2] // parts, act.shape[2] // parts
    span_out, span_in = span(my_part, wide_out), span(my_part, wide_in)
    to_out, to_in = pl.ds(0, wide_out), pl.ds(wide_out, wide_in)
    copies = [
        pltpu.make_async_copy(grad.at[0, :, span_out], rows.at[:, to_out], sem.at[0]),
        pltpu.make_async_copy(act.at[0, :, span_in], rows.at[:, to_in], sem.at[1]),
    ]
    for copy in copies:
        copy.start()
    for table in tables:
        table.wait()
    (row,) = pick_rows(query_row, pairs, per_owner, [my_shard])
    copies += [
        pltpu.make_async_copy(factor_out.at[0, row, :, span_out], slot.at[:, to_out], sem.at[2]),
        pltpu.make_async_copy(factor_in.at[0, row, :, span_in], slot.at[:, to_in], sem.at[3]),
    ]
    for copy in copies[2:]:
        copy.start()
    wide = query_row.shape[0] // layers
    for e in range(layers):
        layer = wrap(my_layer + e, layers)
        for i in range(wide):
            q = layer * wide + i
            listed = pairs[my_layer, my_shard, q]
            for k, j in enumerate(order):
                row = query_row[q] - source(my_shard, j, shard_count) * per_owner
                here = jnp.logical_and(row >= 0, row < per_owner)
                weight = jnp.where(here, listed, 0).astype(jnp.float32)
                weights[e, k, i : i + 1, :] = jnp.full((1, tokens), weight, jnp.float32)
    for copy in copies:
        copy.wait()


def make_own(order, act, grad, factor_in, factor_out, query_row, pairs):
    parts, layers = lax.axis_size("parts"), lax.axis_size("layer")
    rank, tokens = factor_out.shape[2], act.shape[1]
    wide = (grad.shape[2] + act.shape[2]) // parts
    shapes = [
        pltpu.VMEM((tokens, wide), act.dtype),
        pltpu.VMEM((rank, wide), act.dtype),
        pltpu.VMEM((layers, len(order), query_row.shape[0] // layers, tokens), jnp.float32),
    ]
    return pl.pallas_call(
        functools.partial(own_kernel, parts, tuple(order)),
        out_shape=shapes,
        in_specs=[pl.BlockSpec(memory_space=pltpu.HBM)] * 6,
        out_specs=[pl.BlockSpec(memory_space=pltpu.VMEM)] * len(shapes),
        scratch_shapes=table_scratch(query_row, pairs) + [pltpu.SemaphoreType.DMA((4,)), pltpu.SemaphoreType.DMA((2,))],
        compiler_params=pltpu.CompilerParams(vmem_limit_bytes=2**22),
        name="make_own",
    )(query_row, pairs, act, grad, factor_in, factor_out)


def project_kernel(slot_count, block_count, subs, wide_out, *refs):
    slots, blocks, rest = refs[:slot_count], refs[slot_count : slot_count + block_count], refs[slot_count + block_count :]
    carried, outs = rest[: -block_count * subs], rest[-block_count * subs :]
    my_sub = lax.axis_index("sub")
    dims = (((1,), (1,)), ((), ()))
    rank, wide = slots[0].shape
    half = rank // subs
    for out, old in zip(outs, carried):
        out[:, : old.shape[1]] = old[...]
    for which, (low, high) in enumerate(((0, wide_out), (wide_out, wide))):
        left = jnp.concatenate([slot[:, low:high] for slot in slots], axis=0)
        for e, block in enumerate(blocks):
            proj = lax.dot_general(left, block[:, low:high], dims, preferred_element_type=jnp.float32)
            for j in range(slot_count):
                cuts = [proj[j * rank + c * half : j * rank + (c + 1) * half] for c in range(subs)]
                for f in range(subs):
                    sub = wrap(my_sub + f, subs)
                    cut = cuts[0]
                    for c in range(1, subs):
                        cut = jnp.where(sub == c, cuts[c], cut)
                    out = outs[e * subs + f]
                    out[which, out.shape[1] - slot_count + j] = cut


def project(slots, blocks, wide_out, carried=()):
    subs = lax.axis_size("sub")
    vmem = pl.BlockSpec(memory_space=pltpu.VMEM)
    (rank, wide), tokens = slots[0].shape, blocks[0].shape[0]
    counts = [len(slots) + (carried[k].shape[1] if k < len(carried) else 0) for k in range(len(blocks) * subs)]
    inputs = [pltpu.with_memory_space_constraint(x, pltpu.VMEM) for x in (*slots, *blocks, *carried)]
    flops = 2 * len(slots) * rank * len(blocks) * tokens * wide
    read = 2 * wide * (len(slots) * rank + len(blocks) * tokens)
    return pl.pallas_call(
        functools.partial(project_kernel, len(slots), len(blocks), subs, wide_out),
        out_shape=[pltpu.VMEM((2, count, rank // subs, tokens), jnp.float32) for count in counts],
        in_specs=[vmem] * len(inputs),
        out_specs=[vmem] * len(counts),
        compiler_params=pltpu.CompilerParams(vmem_limit_bytes=2**23),
        cost_estimate=pl.CostEstimate(flops=flops, bytes_accessed=read, transcendentals=0),
        name="project",
    )(*inputs)


def score_kernel(counts, weights, *refs):
    pieces, outs = list(refs[: sum(counts)]), refs[sum(counts) :]
    whole = [pieces.pop(0) for _ in range(counts[0])]
    scores = []
    for count in counts[1:]:
        parted = [pieces.pop(0) for _ in range(count)]
        width = parted[0].shape[1]
        total = whole[0][:, len(scores) : len(scores) + width]
        for piece in whole[1:]:
            total = total + piece[:, len(scores) : len(scores) + width]
        for piece in parted:
            total = total + piece[...]
        scores += [jnp.sum(total[0, k] * total[1, k], axis=0, keepdims=True) for k in range(width)]
    for e, out in enumerate(outs):
        block = weights[e, 0] * scores[0]
        for k in range(1, len(scores)):
            block = block + weights[e, k] * scores[k]
        out[...] = block


def make_scores(weights, whole, parted):
    layers, _, wide, tokens = weights.shape
    vmem = pl.BlockSpec(memory_space=pltpu.VMEM)
    pieces = [weights, *whole] + [piece for group in parted for piece in group]
    inputs = [pltpu.with_memory_space_constraint(x, pltpu.VMEM) for x in pieces]
    counts = (len(whole), *[len(group) for group in parted])
    return pl.pallas_call(
        functools.partial(score_kernel, counts),
        out_shape=[pltpu.VMEM((wide, tokens), jnp.float32)] * layers,
        in_specs=[vmem] * len(inputs),
        out_specs=[vmem] * layers,
        compiler_params=pltpu.CompilerParams(vmem_limit_bytes=2**23),
        name="make_scores",
    )(*inputs)


def shards(act_in, grad_out, factor_in, factor_out, query_row, pairs):
    parts = lax.axis_size("parts")
    shard_count = lax.axis_size("shard")
    layers = lax.axis_size("layer")
    subs = lax.axis_size("sub")
    wide_out = grad_out.shape[2] // parts
    early, late = slot_groups(shard_count)

    args = [
        pltpu.with_memory_space_constraint(x, pltpu.HBM)
        for x in (act_in, grad_out, factor_in, factor_out, query_row, pairs)
    ]
    sent_slots, sent_rows = make_sends(*args)
    rows = []
    for e in range(1, parts):
        rows.append(lax.ppermute(sent_rows[e - 1], "parts", shifted((parts,), (e,))))
    slots = [None] * shard_count
    for j in late[::-1] + early[1:]:
        to = [(i, dest(i, j, shard_count)) for i in range(shard_count)]
        slots[j] = lax.ppermute(sent_slots[j - 1], "shard", to)
    own_rows, slots[0], weights = make_own(early + late, *args)

    def give_back(cuts):
        got = []
        for k, cut in enumerate(cuts):
            e, f = 1 + k // subs, k % subs
            got.append(lax.ppermute(cut, ("parts", "sub"), shifted((parts, subs), (parts - e, f))))
        return got

    early_own = project([slots[j] for j in early], [own_rows], wide_out)
    early_rest = project([slots[j] for j in early], rows, wide_out)
    early_got = give_back(early_rest)
    cuts = project([slots[j] for j in late], [own_rows] + rows, wide_out, early_own)
    late_got = give_back(cuts[subs:])
    whole = [cuts[0]]
    for f in range(1, subs):
        whole.append(lax.ppermute(cuts[f], "sub", shifted((subs,), (f,))))
    blocks = make_scores(weights, whole, [early_got, late_got])

    out = None
    for e in range(layers):
        terms = [blocks[0] if e == f == 0 else lax.ppermute(blocks[e], ("layer", "sub"), shifted((layers, subs), (e, f))) for f in range(subs)]
        total = sum(terms[1:], terms[0])
        out = total if out is None else out + total
    return out.T


def solution(mesh):
    in_specs = (
        P("layer", ("parts", "shard"), "sub"),
        P("layer", ("parts", "shard"), "sub"),
        P("layer", "shard", None, "sub"),
        P("layer", "shard", None, "sub"),
        P(),
        P(),
    )
    out_specs = P(("parts", "shard"), "layer")

    return jax.shard_map(shards, mesh=mesh, in_specs=in_specs, out_specs=out_specs, check_vma=False)
```

```python
import functools
import itertools

import jax
import jax.numpy as jnp
from jax import lax
from jax.experimental import pallas as pl
from jax.experimental.pallas import tpu as pltpu
from jax.sharding import PartitionSpec as P


def shifted(sizes, shift):
    places = list(itertools.product(*[range(n) for n in sizes]))
    return [
        (i, places.index(tuple((a + b) % n for a, b, n in zip(place, shift, sizes)))) for i, place in enumerate(places)
    ]


def wrap(i, n):
    return jnp.where(i >= n, i - n, i)


def dest(shard, j, n):
    if n & (n - 1) == 0:
        return shard ^ j
    return (shard + j) % n


def source(shard, j, n):
    if n & (n - 1) == 0:
        return shard ^ j
    return (shard + n - j) % n


def slot_groups(n):
    late = list(range(max(1, n // 2), n))
    return [j for j in range(n) if j not in late], late


def start_tables(query_hbm, pairs_hbm, query_row, pairs, sem):
    copies = [pltpu.make_async_copy(query_hbm, query_row, sem.at[0]), pltpu.make_async_copy(pairs_hbm, pairs, sem.at[1])]
    for copy in copies:
        copy.start()
    return copies


def table_scratch(query_row, pairs):
    return [pltpu.SMEM(query_row.shape, query_row.dtype), pltpu.SMEM(pairs.shape, pairs.dtype)]


def pick_rows(query_row, pairs, per_owner, dests):
    base = lax.axis_index("shard") * per_owner
    layer = lax.axis_index("layer")

    def step(q, rows):
        row = query_row[q] - base
        held = jnp.logical_and(row >= 0, row < per_owner)
        row = jnp.where(held, row, 0)
        return tuple(r + pairs[layer, to, q] * row for r, to in zip(rows, dests))

    count = query_row.shape[0]
    rows = lax.fori_loop(0, count, step, (jnp.int32(0),) * len(dests), unroll=count <= 16)
    return [jnp.clip(row, 0, per_owner - 1) for row in rows]


def span(part, wide):
    return pl.ds(pl.multiple_of(part * wide, 128), wide)


def send_kernel(parts, shard_count, query_hbm, pairs_hbm, act, grad, factor_in, factor_out, *refs):
    sent, (query_row, pairs, stored, sem, table_sem) = refs[:-5], refs[-5:]
    tables = start_tables(query_hbm, pairs_hbm, query_row, pairs, table_sem)
    my_part, my_shard = lax.axis_index("parts"), lax.axis_index("shard")
    wide_out, wide_in = grad.shape[2] // parts, act.shape[2] // parts
    to_out, to_in = pl.ds(0, wide_out), pl.ds(wide_out, wide_in)
    copies = []

    def start(piece, target):
        copies.append(pltpu.make_async_copy(piece, target, sem.at[len(copies)]))
        copies[-1].start()

    start(factor_out.at[0, :, :, span(my_part, wide_out)], stored.at[:, :, to_out])
    start(factor_in.at[0, :, :, span(my_part, wide_in)], stored.at[:, :, to_in])
    for e in range(1, parts):
        part = wrap(my_part + e, parts)
        start(grad.at[0, :, span(part, wide_out)], sent[shard_count - 1 + e - 1].at[:, to_out])
        start(act.at[0, :, span(part, wide_in)], sent[shard_count - 1 + e - 1].at[:, to_in])
    for table in tables:
        table.wait()
    dests = [dest(my_shard, j, shard_count) for j in range(1, shard_count)]
    listed = pick_rows(query_row, pairs, factor_out.shape[1], dests)
    for copy in copies[:2]:
        copy.wait()
    for target, row in zip(sent, listed):
        target[...] = stored[row]
    for copy in copies[2:]:
        copy.wait()


def make_sends(act, grad, factor_in, factor_out, query_row, pairs):
    parts, shard_count = lax.axis_size("parts"), lax.axis_size("shard")
    rank, tokens = factor_out.shape[2], act.shape[1]
    wide = (grad.shape[2] + act.shape[2]) // parts
    shapes = [pltpu.VMEM((rank, wide), act.dtype)] * (shard_count - 1)
    shapes += [pltpu.VMEM((tokens, wide), act.dtype)] * (parts - 1)
    sent = pl.pallas_call(
        functools.partial(send_kernel, parts, shard_count),
        out_shape=shapes,
        in_specs=[pl.BlockSpec(memory_space=pltpu.HBM)] * 6,
        out_specs=[pl.BlockSpec(memory_space=pltpu.VMEM)] * len(shapes),
        scratch_shapes=table_scratch(query_row, pairs)
        + [
            pltpu.VMEM((factor_out.shape[1], rank, wide), act.dtype),
            pltpu.SemaphoreType.DMA((2 * parts,)),
            pltpu.SemaphoreType.DMA((2,)),
        ],
        compiler_params=pltpu.CompilerParams(vmem_limit_bytes=2**23),
        name="make_sends",
    )(query_row, pairs, act, grad, factor_in, factor_out)
    return sent[: shard_count - 1], sent[shard_count - 1 :]


def own_kernel(parts, order, query_hbm, pairs_hbm, act, grad, factor_in, factor_out, rows, slot, weights, *scratch):
    query_row, pairs, sem, table_sem = scratch
    tables = start_tables(query_hbm, pairs_hbm, query_row, pairs, table_sem)
    my_part, my_shard, my_layer = lax.axis_index("parts"), lax.axis_index("shard"), lax.axis_index("layer")
    layers, shard_count = lax.axis_size("layer"), lax.axis_size("shard")
    per_owner, tokens = factor_out.shape[1], rows.shape[0]
    wide_out, wide_in = grad.shape[2] // parts, act.shape[2] // parts
    span_out, span_in = span(my_part, wide_out), span(my_part, wide_in)
    to_out, to_in = pl.ds(0, wide_out), pl.ds(wide_out, wide_in)
    copies = [
        pltpu.make_async_copy(grad.at[0, :, span_out], rows.at[:, to_out], sem.at[0]),
        pltpu.make_async_copy(act.at[0, :, span_in], rows.at[:, to_in], sem.at[1]),
    ]
    for copy in copies:
        copy.start()
    for table in tables:
        table.wait()
    (row,) = pick_rows(query_row, pairs, per_owner, [my_shard])
    copies += [
        pltpu.make_async_copy(factor_out.at[0, row, :, span_out], slot.at[:, to_out], sem.at[2]),
        pltpu.make_async_copy(factor_in.at[0, row, :, span_in], slot.at[:, to_in], sem.at[3]),
    ]
    for copy in copies[2:]:
        copy.start()
    wide = query_row.shape[0] // layers
    for e in range(layers):
        layer = wrap(my_layer + e, layers)
        for i in range(wide):
            q = layer * wide + i
            listed = pairs[my_layer, my_shard, q]
            for k, j in enumerate(order):
                row = query_row[q] - source(my_shard, j, shard_count) * per_owner
                here = jnp.logical_and(row >= 0, row < per_owner)
                weight = jnp.where(here, listed, 0).astype(jnp.float32)
                weights[e, k, i : i + 1, :] = jnp.full((1, tokens), weight, jnp.float32)
    for copy in copies:
        copy.wait()


def make_own(order, act, grad, factor_in, factor_out, query_row, pairs):
    parts, layers = lax.axis_size("parts"), lax.axis_size("layer")
    rank, tokens = factor_out.shape[2], act.shape[1]
    wide = (grad.shape[2] + act.shape[2]) // parts
    shapes = [
        pltpu.VMEM((tokens, wide), act.dtype),
        pltpu.VMEM((rank, wide), act.dtype),
        pltpu.VMEM((layers, len(order), query_row.shape[0] // layers, tokens), jnp.float32),
    ]
    return pl.pallas_call(
        functools.partial(own_kernel, parts, tuple(order)),
        out_shape=shapes,
        in_specs=[pl.BlockSpec(memory_space=pltpu.HBM)] * 6,
        out_specs=[pl.BlockSpec(memory_space=pltpu.VMEM)] * len(shapes),
        scratch_shapes=table_scratch(query_row, pairs) + [pltpu.SemaphoreType.DMA((4,)), pltpu.SemaphoreType.DMA((2,))],
        compiler_params=pltpu.CompilerParams(vmem_limit_bytes=2**22),
        name="make_own",
    )(query_row, pairs, act, grad, factor_in, factor_out)


def cut_ranks(whole, subs):
    my_sub = lax.axis_index("sub")
    half = whole.shape[-2] // subs
    cuts = [whole[..., c * half : (c + 1) * half, :] for c in range(subs)]
    picked = []
    for f in range(subs):
        sub = wrap(my_sub + f, subs)
        cut = cuts[0]
        for c in range(1, subs):
            cut = jnp.where(sub == c, cuts[c], cut)
        picked.append(cut)
    return picked


def project_kernel(slot_count, block_count, subs, wide_out, *refs):
    slots, blocks, outs = refs[:slot_count], refs[slot_count : slot_count + block_count], refs[slot_count + block_count :]
    dims = (((1,), (1,)), ((), ()))
    rank, wide = slots[0].shape
    for which, (low, high) in enumerate(((0, wide_out), (wide_out, wide))):
        left = jnp.concatenate([slot[:, low:high] for slot in slots], axis=0)
        for e, block in enumerate(blocks):
            proj = lax.dot_general(left, block[:, low:high], dims, preferred_element_type=jnp.float32)
            for j in range(slot_count):
                cuts = cut_ranks(proj[j * rank : (j + 1) * rank], subs)
                for f, cut in enumerate(cuts):
                    outs[e * subs + f][which, j] = cut


def project(slots, blocks, wide_out, subs):
    vmem = pl.BlockSpec(memory_space=pltpu.VMEM)
    (rank, wide), tokens = slots[0].shape, blocks[0].shape[0]
    inputs = [pltpu.with_memory_space_constraint(x, pltpu.VMEM) for x in (*slots, *blocks)]
    flops = 2 * len(slots) * rank * len(blocks) * tokens * wide
    read = 2 * wide * (len(slots) * rank + len(blocks) * tokens)
    count = len(blocks) * subs
    return pl.pallas_call(
        functools.partial(project_kernel, len(slots), len(blocks), subs, wide_out),
        out_shape=[pltpu.VMEM((2, len(slots), rank // subs, tokens), jnp.float32)] * count,
        in_specs=[vmem] * len(inputs),
        out_specs=[vmem] * count,
        compiler_params=pltpu.CompilerParams(vmem_limit_bytes=2**23),
        cost_estimate=pl.CostEstimate(flops=flops, bytes_accessed=read, transcendentals=0),
        name="project",
    )(*inputs)


def join_kernel(count, *refs):
    early, late, outs = refs[:count], refs[count : count + len(refs[count:]) // 2], refs[count + len(refs[count:]) // 2 :]
    total = early[0][...]
    for piece in early[1:]:
        total = total + piece[...]
    split = total.shape[1]
    for out, cut, rest in zip(outs, cut_ranks(total, len(outs)), late):
        out[:, :split] = cut
        out[:, split:] = rest[...]


def join(early, late):
    vmem = pl.BlockSpec(memory_space=pltpu.VMEM)
    inputs = [pltpu.with_memory_space_constraint(x, pltpu.VMEM) for x in (*early, *late)]
    _, count, half, tokens = late[0].shape
    return pl.pallas_call(
        functools.partial(join_kernel, len(early)),
        out_shape=[pltpu.VMEM((2, early[0].shape[1] + count, half, tokens), jnp.float32)] * len(late),
        in_specs=[vmem] * len(inputs),
        out_specs=[vmem] * len(late),
        compiler_params=pltpu.CompilerParams(vmem_limit_bytes=2**23),
        name="join",
    )(*inputs)


def score_kernel(done, whole_count, weights, *refs):
    layers = weights.shape[0]
    pieces, outs = refs[:-layers], refs[-layers:]
    whole, parted = pieces[:whole_count], pieces[whole_count:]
    total = whole[0][...]
    for piece in whole[1:]:
        total = total + piece[...]
    first, last = total[:, :done], total[:, done:]
    for piece in parted:
        last = last + piece[...]
    scores = [jnp.sum(t[0, k] * t[1, k], axis=0, keepdims=True) for t in (first, last) for k in range(t.shape[1])]
    for e, out in enumerate(outs):
        block = weights[e, 0] * scores[0]
        for k in range(1, len(scores)):
            block = block + weights[e, k] * scores[k]
        out[...] = block


def make_scores(weights, whole, parted):
    layers, count, wide, tokens = weights.shape
    vmem = pl.BlockSpec(memory_space=pltpu.VMEM)
    inputs = [pltpu.with_memory_space_constraint(x, pltpu.VMEM) for x in (weights, *whole, *parted)]
    done = count - (parted[0].shape[1] if parted else 0)
    return pl.pallas_call(
        functools.partial(score_kernel, done, len(whole)),
        out_shape=[pltpu.VMEM((wide, tokens), jnp.float32)] * layers,
        in_specs=[vmem] * len(inputs),
        out_specs=[vmem] * layers,
        compiler_params=pltpu.CompilerParams(vmem_limit_bytes=2**23),
        name="make_scores",
    )(*inputs)


def shards(act_in, grad_out, factor_in, factor_out, query_row, pairs):
    parts = lax.axis_size("parts")
    shard_count = lax.axis_size("shard")
    layers = lax.axis_size("layer")
    subs = lax.axis_size("sub")
    wide_out = grad_out.shape[2] // parts
    early, late = slot_groups(shard_count)

    args = [
        pltpu.with_memory_space_constraint(x, pltpu.HBM)
        for x in (act_in, grad_out, factor_in, factor_out, query_row, pairs)
    ]
    sent_slots, sent_rows = make_sends(*args)
    rows = []
    for e in range(1, parts):
        rows.append(lax.ppermute(sent_rows[e - 1], "parts", shifted((parts,), (e,))))
    slots = [None] * shard_count
    for j in late[::-1] + early[1:]:
        to = [(i, dest(i, j, shard_count)) for i in range(shard_count)]
        slots[j] = lax.ppermute(sent_slots[j - 1], "shard", to)
    own_rows, slots[0], weights = make_own(early + late, *args)

    early_own = project([slots[j] for j in early], [own_rows], wide_out, 1)
    early_rest = project([slots[j] for j in early], rows, wide_out, 1)
    early_got = []
    for e, block in enumerate(early_rest, 1):
        early_got.append(lax.ppermute(block, "parts", shifted((parts,), (parts - e,))))
    cuts = project([slots[j] for j in late], [own_rows] + rows, wide_out, subs)
    late_got = []
    for k, cut in enumerate(cuts[subs:]):
        e, f = 1 + k // subs, k % subs
        late_got.append(lax.ppermute(cut, ("parts", "sub"), shifted((parts, subs), (parts - e, f))))
    whole = list(join(list(early_own) + early_got, cuts[:subs]))
    for f in range(1, subs):
        whole[f] = lax.ppermute(whole[f], "sub", shifted((subs,), (f,)))
    blocks = make_scores(weights, whole, late_got)

    out = None
    for e in range(layers):
        terms = [blocks[0] if e == f == 0 else lax.ppermute(blocks[e], ("layer", "sub"), shifted((layers, subs), (e, f))) for f in range(subs)]
        total = sum(terms[1:], terms[0])
        out = total if out is None else out + total
    return out.T


def solution(mesh):
    in_specs = (
        P("layer", ("parts", "shard"), "sub"),
        P("layer", ("parts", "shard"), "sub"),
        P("layer", "shard", None, "sub"),
        P("layer", "shard", None, "sub"),
        P(),
        P(),
    )
    out_specs = P(("parts", "shard"), "layer")

    return jax.shard_map(shards, mesh=mesh, in_specs=in_specs, out_specs=out_specs, check_vma=False)
```

```python
import functools
import itertools

import jax
import jax.numpy as jnp
from jax import lax
from jax.experimental import pallas as pl
from jax.experimental.pallas import tpu as pltpu
from jax.sharding import PartitionSpec as P


def shifted(sizes, shift):
    places = list(itertools.product(*[range(n) for n in sizes]))
    return [
        (i, places.index(tuple((a + b) % n for a, b, n in zip(place, shift, sizes)))) for i, place in enumerate(places)
    ]


def wrap(i, n):
    return jnp.where(i >= n, i - n, i)


def dest(shard, j, n):
    if n & (n - 1) == 0:
        return shard ^ j
    return (shard + j) % n


def source(shard, j, n):
    if n & (n - 1) == 0:
        return shard ^ j
    return (shard + n - j) % n


def slot_groups(n):
    late = list(range(max(1, n // 2), n))
    return [j for j in range(n) if j not in late], late


def start_tables(query_hbm, pairs_hbm, query_row, pairs, sem):
    copies = [pltpu.make_async_copy(query_hbm, query_row, sem.at[0]), pltpu.make_async_copy(pairs_hbm, pairs, sem.at[1])]
    for copy in copies:
        copy.start()
    return copies


def table_scratch(query_row, pairs):
    return [pltpu.SMEM(query_row.shape, query_row.dtype), pltpu.SMEM(pairs.shape, pairs.dtype)]


def pick_rows(query_row, pairs, per_owner, dests):
    base = lax.axis_index("shard") * per_owner
    layer = lax.axis_index("layer")

    def step(q, rows):
        row = query_row[q] - base
        held = jnp.logical_and(row >= 0, row < per_owner)
        row = jnp.where(held, row, 0)
        return tuple(r + pairs[layer, to, q] * row for r, to in zip(rows, dests))

    count = query_row.shape[0]
    rows = lax.fori_loop(0, count, step, (jnp.int32(0),) * len(dests), unroll=count <= 16)
    return [jnp.clip(row, 0, per_owner - 1) for row in rows]


def span(part, wide):
    return pl.ds(pl.multiple_of(part * wide, 128), wide)


def send_kernel(parts, shard_count, query_hbm, pairs_hbm, act, grad, factor_in, factor_out, *refs):
    sent, (query_row, pairs, stored, sem, table_sem) = refs[:-5], refs[-5:]
    tables = start_tables(query_hbm, pairs_hbm, query_row, pairs, table_sem)
    my_part, my_shard = lax.axis_index("parts"), lax.axis_index("shard")
    wide_out, wide_in = grad.shape[2] // parts, act.shape[2] // parts
    to_out, to_in = pl.ds(0, wide_out), pl.ds(wide_out, wide_in)
    copies = []

    def start(piece, target):
        copies.append(pltpu.make_async_copy(piece, target, sem.at[len(copies)]))
        copies[-1].start()

    start(factor_out.at[0, :, :, span(my_part, wide_out)], stored.at[:, :, to_out])
    start(factor_in.at[0, :, :, span(my_part, wide_in)], stored.at[:, :, to_in])
    for e in range(1, parts):
        part = wrap(my_part + e, parts)
        start(grad.at[0, :, span(part, wide_out)], sent[shard_count - 1 + e - 1].at[:, to_out])
        start(act.at[0, :, span(part, wide_in)], sent[shard_count - 1 + e - 1].at[:, to_in])
    for table in tables:
        table.wait()
    dests = [dest(my_shard, j, shard_count) for j in range(1, shard_count)]
    listed = pick_rows(query_row, pairs, factor_out.shape[1], dests)
    for copy in copies[:2]:
        copy.wait()
    for target, row in zip(sent, listed):
        target[...] = stored[row]
    for copy in copies[2:]:
        copy.wait()


def make_sends(act, grad, factor_in, factor_out, query_row, pairs):
    parts, shard_count = lax.axis_size("parts"), lax.axis_size("shard")
    rank, tokens = factor_out.shape[2], act.shape[1]
    wide = (grad.shape[2] + act.shape[2]) // parts
    shapes = [pltpu.VMEM((rank, wide), act.dtype)] * (shard_count - 1)
    shapes += [pltpu.VMEM((tokens, wide), act.dtype)] * (parts - 1)
    sent = pl.pallas_call(
        functools.partial(send_kernel, parts, shard_count),
        out_shape=shapes,
        in_specs=[pl.BlockSpec(memory_space=pltpu.HBM)] * 6,
        out_specs=[pl.BlockSpec(memory_space=pltpu.VMEM)] * len(shapes),
        scratch_shapes=table_scratch(query_row, pairs)
        + [
            pltpu.VMEM((factor_out.shape[1], rank, wide), act.dtype),
            pltpu.SemaphoreType.DMA((2 * parts,)),
            pltpu.SemaphoreType.DMA((2,)),
        ],
        compiler_params=pltpu.CompilerParams(vmem_limit_bytes=2**23),
        name="make_sends",
    )(query_row, pairs, act, grad, factor_in, factor_out)
    return sent[: shard_count - 1], sent[shard_count - 1 :]


def own_kernel(parts, order, query_hbm, pairs_hbm, act, grad, factor_in, factor_out, rows, slot, weights, *scratch):
    query_row, pairs, sem, table_sem = scratch
    tables = start_tables(query_hbm, pairs_hbm, query_row, pairs, table_sem)
    my_part, my_shard, my_layer = lax.axis_index("parts"), lax.axis_index("shard"), lax.axis_index("layer")
    layers, shard_count = lax.axis_size("layer"), lax.axis_size("shard")
    per_owner, tokens = factor_out.shape[1], rows.shape[0]
    wide_out, wide_in = grad.shape[2] // parts, act.shape[2] // parts
    span_out, span_in = span(my_part, wide_out), span(my_part, wide_in)
    to_out, to_in = pl.ds(0, wide_out), pl.ds(wide_out, wide_in)
    copies = [
        pltpu.make_async_copy(grad.at[0, :, span_out], rows.at[:, to_out], sem.at[0]),
        pltpu.make_async_copy(act.at[0, :, span_in], rows.at[:, to_in], sem.at[1]),
    ]
    for copy in copies:
        copy.start()
    for table in tables:
        table.wait()
    (row,) = pick_rows(query_row, pairs, per_owner, [my_shard])
    copies += [
        pltpu.make_async_copy(factor_out.at[0, row, :, span_out], slot.at[:, to_out], sem.at[2]),
        pltpu.make_async_copy(factor_in.at[0, row, :, span_in], slot.at[:, to_in], sem.at[3]),
    ]
    for copy in copies[2:]:
        copy.start()
    wide = query_row.shape[0] // layers
    for e in range(layers):
        layer = wrap(my_layer + e, layers)
        for i in range(wide):
            q = layer * wide + i
            listed = pairs[my_layer, my_shard, q]
            for k, j in enumerate(order):
                row = query_row[q] - source(my_shard, j, shard_count) * per_owner
                here = jnp.logical_and(row >= 0, row < per_owner)
                weight = jnp.where(here, listed, 0).astype(jnp.float32)
                weights[e, k, i : i + 1, :] = jnp.full((1, tokens), weight, jnp.float32)
    for copy in copies:
        copy.wait()


def make_own(order, act, grad, factor_in, factor_out, query_row, pairs):
    parts, layers = lax.axis_size("parts"), lax.axis_size("layer")
    rank, tokens = factor_out.shape[2], act.shape[1]
    wide = (grad.shape[2] + act.shape[2]) // parts
    shapes = [
        pltpu.VMEM((tokens, wide), act.dtype),
        pltpu.VMEM((rank, wide), act.dtype),
        pltpu.VMEM((layers, len(order), query_row.shape[0] // layers, tokens), jnp.float32),
    ]
    return pl.pallas_call(
        functools.partial(own_kernel, parts, tuple(order)),
        out_shape=shapes,
        in_specs=[pl.BlockSpec(memory_space=pltpu.HBM)] * 6,
        out_specs=[pl.BlockSpec(memory_space=pltpu.VMEM)] * len(shapes),
        scratch_shapes=table_scratch(query_row, pairs) + [pltpu.SemaphoreType.DMA((4,)), pltpu.SemaphoreType.DMA((2,))],
        compiler_params=pltpu.CompilerParams(vmem_limit_bytes=2**22),
        name="make_own",
    )(query_row, pairs, act, grad, factor_in, factor_out)


def project_kernel(slot_count, wide_out, *refs):
    slots, rest = refs[:slot_count], refs[slot_count:]
    blocks, outs = rest[: len(rest) // 2], rest[len(rest) // 2 :]
    dims = (((1,), (1,)), ((), ()))
    rank, wide = slots[0].shape
    for which, (low, high) in enumerate(((0, wide_out), (wide_out, wide))):
        left = jnp.concatenate([slot[:, low:high] for slot in slots], axis=0)
        for block, out in zip(blocks, outs):
            proj = lax.dot_general(left, block[:, low:high], dims, preferred_element_type=jnp.float32)
            for j in range(slot_count):
                out[which, j] = proj[j * rank : (j + 1) * rank]


def project(slots, blocks, wide_out):
    vmem = pl.BlockSpec(memory_space=pltpu.VMEM)
    (rank, wide), tokens = slots[0].shape, blocks[0].shape[0]
    inputs = [pltpu.with_memory_space_constraint(x, pltpu.VMEM) for x in (*slots, *blocks)]
    flops = 2 * len(slots) * rank * len(blocks) * tokens * wide
    read = 2 * wide * (len(slots) * rank + len(blocks) * tokens)
    return pl.pallas_call(
        functools.partial(project_kernel, len(slots), wide_out),
        out_shape=[pltpu.VMEM((2, len(slots), rank, tokens), jnp.float32)] * len(blocks),
        in_specs=[vmem] * len(inputs),
        out_specs=[vmem] * len(blocks),
        compiler_params=pltpu.CompilerParams(vmem_limit_bytes=2**23),
        cost_estimate=pl.CostEstimate(flops=flops, bytes_accessed=read, transcendentals=0),
        name="project",
    )(*inputs)


def join_kernel(*refs):
    early, late, out = refs[:-2], refs[-2], refs[-1]
    total = early[0][...]
    for piece in early[1:]:
        total = total + piece[...]
    out[:, : total.shape[1]] = total
    out[:, total.shape[1] :] = late[...]


def join(early, late):
    vmem = pl.BlockSpec(memory_space=pltpu.VMEM)
    inputs = [pltpu.with_memory_space_constraint(x, pltpu.VMEM) for x in (*early, late)]
    return pl.pallas_call(
        join_kernel,
        out_shape=pltpu.VMEM((2, early[0].shape[1] + late.shape[1], *late.shape[2:]), jnp.float32),
        in_specs=[vmem] * len(inputs),
        out_specs=vmem,
        compiler_params=pltpu.CompilerParams(vmem_limit_bytes=2**23),
        name="join",
    )(*inputs)


def score_kernel(done, whole_count, weights, *refs):
    layers = weights.shape[0]
    pieces, outs = refs[:-layers], refs[-layers:]
    whole, parted = pieces[:whole_count], pieces[whole_count:]
    total = whole[0][...]
    for piece in whole[1:]:
        total = total + piece[...]
    first, last = total[:, :done], total[:, done:]
    if parted:
        more = parted[0][...]
        for piece in parted[1:]:
            more = more + piece[...]
        last = last + more
    scores = [jnp.sum(t[0, k] * t[1, k], axis=0, keepdims=True) for t in (first, last) for k in range(t.shape[1])]
    for e, out in enumerate(outs):
        block = weights[e, 0] * scores[0]
        for k in range(1, len(scores)):
            block = block + weights[e, k] * scores[k]
        out[...] = block


def make_scores(weights, whole, parted):
    layers, count, wide, tokens = weights.shape
    vmem = pl.BlockSpec(memory_space=pltpu.VMEM)
    inputs = [pltpu.with_memory_space_constraint(x, pltpu.VMEM) for x in (weights, *whole, *parted)]
    done = count - (parted[0].shape[1] if parted else 0)
    return pl.pallas_call(
        functools.partial(score_kernel, done, len(whole)),
        out_shape=[pltpu.VMEM((wide, tokens), jnp.float32)] * layers,
        in_specs=[vmem] * len(inputs),
        out_specs=[vmem] * layers,
        compiler_params=pltpu.CompilerParams(vmem_limit_bytes=2**23),
        name="make_scores",
    )(*inputs)


def shards(act_in, grad_out, factor_in, factor_out, query_row, pairs):
    parts = lax.axis_size("parts")
    shard_count = lax.axis_size("shard")
    layers = lax.axis_size("layer")
    subs = lax.axis_size("sub")
    wide_out = grad_out.shape[2] // parts
    early, late = slot_groups(shard_count)

    args = [
        pltpu.with_memory_space_constraint(x, pltpu.HBM)
        for x in (act_in, grad_out, factor_in, factor_out, query_row, pairs)
    ]
    sent_slots, sent_rows = make_sends(*args)
    rows = []
    for e in range(1, parts):
        rows.append(lax.ppermute(sent_rows[e - 1], "parts", shifted((parts,), (e,))))
    slots = [None] * shard_count
    for j in late[::-1] + early[1:]:
        to = [(i, dest(i, j, shard_count)) for i in range(shard_count)]
        slots[j] = lax.ppermute(sent_slots[j - 1], "shard", to)
    own_rows, slots[0], weights = make_own(early + late, *args)

    early_own = project([slots[j] for j in early], [own_rows], wide_out)
    early_rest = project([slots[j] for j in early], rows, wide_out) if rows else []
    early_got, late_got = [], []
    for e, block in enumerate(early_rest, 1):
        early_got.append(lax.ppermute(block, "parts", shifted((parts,), (parts - e,))))
    late_rest = project([slots[j] for j in late], rows, wide_out) if rows else []
    for e, block in enumerate(late_rest, 1):
        for f in range(subs):
            late_got.append(lax.ppermute(block, ("parts", "sub"), shifted((parts, subs), (parts - e, f))))
    (late_own,) = project([slots[j] for j in late], [own_rows], wide_out)
    whole = [join(list(early_own) + early_got, late_own)]
    for f in range(1, subs):
        whole.append(lax.ppermute(whole[0], "sub", shifted((subs,), (f,))))
    blocks = make_scores(weights, whole, late_got)

    out = blocks[0]
    for e in range(1, layers):
        out = out + lax.ppermute(blocks[e], "layer", shifted((layers,), (e,)))
    return out.T


def solution(mesh):
    in_specs = (
        P("layer", ("parts", "shard"), "sub"),
        P("layer", ("parts", "shard"), "sub"),
        P("layer", "shard", None, "sub"),
        P("layer", "shard", None, "sub"),
        P(),
        P(),
    )
    out_specs = P(("parts", "shard"), "layer")

    return jax.shard_map(shards, mesh=mesh, in_specs=in_specs, out_specs=out_specs, check_vma=False)
```

```python
import functools
import itertools

import jax
import jax.numpy as jnp
from jax import lax
from jax.experimental import pallas as pl
from jax.experimental.pallas import tpu as pltpu
from jax.sharding import PartitionSpec as P


def shifted(sizes, shift):
    places = list(itertools.product(*[range(n) for n in sizes]))
    return [
        (i, places.index(tuple((a + b) % n for a, b, n in zip(place, shift, sizes)))) for i, place in enumerate(places)
    ]


def wrap(i, n):
    return jnp.where(i >= n, i - n, i)


def dest(shard, j, n):
    if n & (n - 1) == 0:
        return shard ^ j
    return (shard + j) % n


def source(shard, j, n):
    if n & (n - 1) == 0:
        return shard ^ j
    return (shard + n - j) % n


def slot_groups(n):
    late = [n // 2] if n > 1 else []
    return [j for j in range(n) if j not in late], late


def start_order(n):
    return list(range(n - 1, n // 2 - 1, -1)) + list(range(1, n // 2))


def start_tables(query_hbm, pairs_hbm, query_row, pairs, sem):
    copies = [pltpu.make_async_copy(query_hbm, query_row, sem.at[0]), pltpu.make_async_copy(pairs_hbm, pairs, sem.at[1])]
    for copy in copies:
        copy.start()
    return copies


def table_scratch(query_row, pairs):
    return [pltpu.SMEM(query_row.shape, query_row.dtype), pltpu.SMEM(pairs.shape, pairs.dtype)]


def pick_rows(query_row, pairs, per_owner, dests):
    base = lax.axis_index("shard") * per_owner
    layer = lax.axis_index("layer")

    def step(q, rows):
        row = query_row[q] - base
        held = jnp.logical_and(row >= 0, row < per_owner)
        row = jnp.where(held, row, 0)
        return tuple(r + pairs[layer, to, q] * row for r, to in zip(rows, dests))

    count = query_row.shape[0]
    rows = lax.fori_loop(0, count, step, (jnp.int32(0),) * len(dests), unroll=count <= 16)
    return [jnp.clip(row, 0, per_owner - 1) for row in rows]


def span(part, wide):
    return pl.ds(pl.multiple_of(part * wide, 128), wide)


def send_kernel(parts, shard_count, query_hbm, pairs_hbm, act, grad, factor_in, factor_out, *refs):
    sent, (query_row, pairs, stored, sem, table_sem) = refs[:-5], refs[-5:]
    tables = start_tables(query_hbm, pairs_hbm, query_row, pairs, table_sem)
    my_part, my_shard = lax.axis_index("parts"), lax.axis_index("shard")
    wide_out, wide_in = grad.shape[2] // parts, act.shape[2] // parts
    to_out, to_in = pl.ds(0, wide_out), pl.ds(wide_out, wide_in)
    copies = []

    def start(piece, target):
        copies.append(pltpu.make_async_copy(piece, target, sem.at[len(copies)]))
        copies[-1].start()

    start(factor_out.at[0, :, :, span(my_part, wide_out)], stored.at[:, :, to_out])
    start(factor_in.at[0, :, :, span(my_part, wide_in)], stored.at[:, :, to_in])
    for e in range(1, parts):
        part = wrap(my_part + e, parts)
        start(grad.at[0, :, span(part, wide_out)], sent[shard_count - 1 + e - 1].at[:, to_out])
        start(act.at[0, :, span(part, wide_in)], sent[shard_count - 1 + e - 1].at[:, to_in])
    for table in tables:
        table.wait()
    dests = [dest(my_shard, j, shard_count) for j in range(1, shard_count)]
    listed = pick_rows(query_row, pairs, factor_out.shape[1], dests)
    for copy in copies[:2]:
        copy.wait()
    for target, row in zip(sent, listed):
        target[...] = stored[row]
    for copy in copies[2:]:
        copy.wait()


def make_sends(act, grad, factor_in, factor_out, query_row, pairs):
    parts, shard_count = lax.axis_size("parts"), lax.axis_size("shard")
    rank, tokens = factor_out.shape[2], act.shape[1]
    wide = (grad.shape[2] + act.shape[2]) // parts
    shapes = [pltpu.VMEM((rank, wide), act.dtype)] * (shard_count - 1)
    shapes += [pltpu.VMEM((tokens, wide), act.dtype)] * (parts - 1)
    sent = pl.pallas_call(
        functools.partial(send_kernel, parts, shard_count),
        out_shape=shapes,
        in_specs=[pl.BlockSpec(memory_space=pltpu.HBM)] * 6,
        out_specs=[pl.BlockSpec(memory_space=pltpu.VMEM)] * len(shapes),
        scratch_shapes=table_scratch(query_row, pairs)
        + [
            pltpu.VMEM((factor_out.shape[1], rank, wide), act.dtype),
            pltpu.SemaphoreType.DMA((2 * parts,)),
            pltpu.SemaphoreType.DMA((2,)),
        ],
        compiler_params=pltpu.CompilerParams(vmem_limit_bytes=2**23),
        name="make_sends",
    )(query_row, pairs, act, grad, factor_in, factor_out)
    return sent[: shard_count - 1], sent[shard_count - 1 :]


def own_kernel(parts, order, query_hbm, pairs_hbm, act, grad, factor_in, factor_out, rows, slot, weights, *scratch):
    query_row, pairs, sem, table_sem = scratch
    tables = start_tables(query_hbm, pairs_hbm, query_row, pairs, table_sem)
    my_part, my_shard, my_layer = lax.axis_index("parts"), lax.axis_index("shard"), lax.axis_index("layer")
    layers, shard_count = lax.axis_size("layer"), lax.axis_size("shard")
    per_owner, tokens = factor_out.shape[1], rows.shape[0]
    wide_out, wide_in = grad.shape[2] // parts, act.shape[2] // parts
    span_out, span_in = span(my_part, wide_out), span(my_part, wide_in)
    to_out, to_in = pl.ds(0, wide_out), pl.ds(wide_out, wide_in)
    copies = [
        pltpu.make_async_copy(grad.at[0, :, span_out], rows.at[:, to_out], sem.at[0]),
        pltpu.make_async_copy(act.at[0, :, span_in], rows.at[:, to_in], sem.at[1]),
    ]
    for copy in copies:
        copy.start()
    for table in tables:
        table.wait()
    (row,) = pick_rows(query_row, pairs, per_owner, [my_shard])
    copies += [
        pltpu.make_async_copy(factor_out.at[0, row, :, span_out], slot.at[:, to_out], sem.at[2]),
        pltpu.make_async_copy(factor_in.at[0, row, :, span_in], slot.at[:, to_in], sem.at[3]),
    ]
    for copy in copies[2:]:
        copy.start()
    wide = query_row.shape[0] // layers
    for e in range(layers):
        layer = wrap(my_layer + e, layers)
        for i in range(wide):
            q = layer * wide + i
            listed = pairs[my_layer, my_shard, q]
            for k, j in enumerate(order):
                row = query_row[q] - source(my_shard, j, shard_count) * per_owner
                here = jnp.logical_and(row >= 0, row < per_owner)
                weight = jnp.where(here, listed, 0).astype(jnp.float32)
                weights[e, k, i : i + 1, :] = jnp.full((1, tokens), weight, jnp.float32)
    for copy in copies:
        copy.wait()


def make_own(order, act, grad, factor_in, factor_out, query_row, pairs):
    parts, layers = lax.axis_size("parts"), lax.axis_size("layer")
    rank, tokens = factor_out.shape[2], act.shape[1]
    wide = (grad.shape[2] + act.shape[2]) // parts
    shapes = [
        pltpu.VMEM((tokens, wide), act.dtype),
        pltpu.VMEM((rank, wide), act.dtype),
        pltpu.VMEM((layers, len(order), query_row.shape[0] // layers, tokens), jnp.float32),
    ]
    return pl.pallas_call(
        functools.partial(own_kernel, parts, tuple(order)),
        out_shape=shapes,
        in_specs=[pl.BlockSpec(memory_space=pltpu.HBM)] * 6,
        out_specs=[pl.BlockSpec(memory_space=pltpu.VMEM)] * len(shapes),
        scratch_shapes=table_scratch(query_row, pairs) + [pltpu.SemaphoreType.DMA((4,)), pltpu.SemaphoreType.DMA((2,))],
        compiler_params=pltpu.CompilerParams(vmem_limit_bytes=2**22),
        name="make_own",
    )(query_row, pairs, act, grad, factor_in, factor_out)


def project_kernel(slot_count, wide_out, *refs):
    slots, rest = refs[:slot_count], refs[slot_count:]
    blocks, outs = rest[: len(rest) // 2], rest[len(rest) // 2 :]
    dims = (((1,), (1,)), ((), ()))
    rank, wide = slots[0].shape
    for which, (low, high) in enumerate(((0, wide_out), (wide_out, wide))):
        left = jnp.concatenate([slot[:, low:high] for slot in slots], axis=0)
        for block, out in zip(blocks, outs):
            proj = lax.dot_general(left, block[:, low:high], dims, preferred_element_type=jnp.float32)
            for j in range(slot_count):
                out[which, j] = proj[j * rank : (j + 1) * rank]


def project(slots, blocks, wide_out):
    vmem = pl.BlockSpec(memory_space=pltpu.VMEM)
    (rank, wide), tokens = slots[0].shape, blocks[0].shape[0]
    inputs = [pltpu.with_memory_space_constraint(x, pltpu.VMEM) for x in (*slots, *blocks)]
    flops = 2 * len(slots) * rank * len(blocks) * tokens * wide
    read = 2 * wide * (len(slots) * rank + len(blocks) * tokens)
    return pl.pallas_call(
        functools.partial(project_kernel, len(slots), wide_out),
        out_shape=[pltpu.VMEM((2, len(slots), rank, tokens), jnp.float32)] * len(blocks),
        in_specs=[vmem] * len(inputs),
        out_specs=[vmem] * len(blocks),
        compiler_params=pltpu.CompilerParams(vmem_limit_bytes=2**23),
        cost_estimate=pl.CostEstimate(flops=flops, bytes_accessed=read, transcendentals=0),
        name="project",
    )(*inputs)


def join_kernel(*refs):
    early, late, out = refs[:-2], refs[-2], refs[-1]
    total = early[0][...]
    for piece in early[1:]:
        total = total + piece[...]
    out[:, : total.shape[1]] = total
    out[:, total.shape[1] :] = late[...]


def join(early, late):
    vmem = pl.BlockSpec(memory_space=pltpu.VMEM)
    inputs = [pltpu.with_memory_space_constraint(x, pltpu.VMEM) for x in (*early, late)]
    return pl.pallas_call(
        join_kernel,
        out_shape=pltpu.VMEM((2, early[0].shape[1] + late.shape[1], *late.shape[2:]), jnp.float32),
        in_specs=[vmem] * len(inputs),
        out_specs=vmem,
        compiler_params=pltpu.CompilerParams(vmem_limit_bytes=2**23),
        name="join",
    )(*inputs)


def score_kernel(done, whole_count, weights, *refs):
    layers = weights.shape[0]
    pieces, outs = refs[:-layers], refs[-layers:]
    whole, parted = pieces[:whole_count], pieces[whole_count:]
    total = whole[0][...]
    for piece in whole[1:]:
        total = total + piece[...]
    first, last = total[:, :done], total[:, done:]
    if parted:
        more = parted[0][...]
        for piece in parted[1:]:
            more = more + piece[...]
        last = last + more
    scores = [jnp.sum(t[0, k] * t[1, k], axis=0, keepdims=True) for t in (first, last) for k in range(t.shape[1])]
    for e, out in enumerate(outs):
        block = weights[e, 0] * scores[0]
        for k in range(1, len(scores)):
            block = block + weights[e, k] * scores[k]
        out[...] = block


def make_scores(weights, whole, parted):
    layers, count, wide, tokens = weights.shape
    vmem = pl.BlockSpec(memory_space=pltpu.VMEM)
    inputs = [pltpu.with_memory_space_constraint(x, pltpu.VMEM) for x in (weights, *whole, *parted)]
    done = count - (parted[0].shape[1] if parted else 0)
    return pl.pallas_call(
        functools.partial(score_kernel, done, len(whole)),
        out_shape=[pltpu.VMEM((wide, tokens), jnp.float32)] * layers,
        in_specs=[vmem] * len(inputs),
        out_specs=[vmem] * layers,
        compiler_params=pltpu.CompilerParams(vmem_limit_bytes=2**23),
        name="make_scores",
    )(*inputs)


def shards(act_in, grad_out, factor_in, factor_out, query_row, pairs):
    parts = lax.axis_size("parts")
    shard_count = lax.axis_size("shard")
    layers = lax.axis_size("layer")
    subs = lax.axis_size("sub")
    wide_out = grad_out.shape[2] // parts
    early, late = slot_groups(shard_count)

    args = [
        pltpu.with_memory_space_constraint(x, pltpu.HBM)
        for x in (act_in, grad_out, factor_in, factor_out, query_row, pairs)
    ]
    sent_slots, sent_rows = make_sends(*args)
    rows = []
    for e in range(1, parts):
        rows.append(lax.ppermute(sent_rows[e - 1], "parts", shifted((parts,), (e,))))
    slots = [None] * shard_count
    for j in start_order(shard_count):
        to = [(i, dest(i, j, shard_count)) for i in range(shard_count)]
        slots[j] = lax.ppermute(sent_slots[j - 1], "shard", to)
    own_rows, slots[0], weights = make_own(early + late, *args)

    early_own = project([slots[j] for j in early], [own_rows], wide_out)
    early_rest = project([slots[j] for j in early], rows, wide_out) if rows else []
    early_got, late_got = [], []
    for e, block in enumerate(early_rest, 1):
        early_got.append(lax.ppermute(block, "parts", shifted((parts,), (parts - e,))))
    late_rest = project([slots[j] for j in late], rows, wide_out) if rows else []
    for e, block in enumerate(late_rest, 1):
        for f in range(subs):
            late_got.append(lax.ppermute(block, ("parts", "sub"), shifted((parts, subs), (parts - e, f))))
    (late_own,) = project([slots[j] for j in late], [own_rows], wide_out)
    whole = [join(list(early_own) + early_got, late_own)]
    for f in range(1, subs):
        whole.append(lax.ppermute(whole[0], "sub", shifted((subs,), (f,))))
    blocks = make_scores(weights, whole, late_got)

    out = blocks[0]
    for e in range(1, layers):
        out = out + lax.ppermute(blocks[e], "layer", shifted((layers,), (e,)))
    return out.T


def solution(mesh):
    in_specs = (
        P("layer", ("parts", "shard"), "sub"),
        P("layer", ("parts", "shard"), "sub"),
        P("layer", "shard", None, "sub"),
        P("layer", "shard", None, "sub"),
        P(),
        P(),
    )
    out_specs = P(("parts", "shard"), "layer")

    return jax.shard_map(shards, mesh=mesh, in_specs=in_specs, out_specs=out_specs, check_vma=False)
```

```python
import functools
import itertools

import jax
import jax.numpy as jnp
from jax import lax
from jax.experimental import pallas as pl
from jax.experimental.pallas import tpu as pltpu
from jax.sharding import PartitionSpec as P


def shifted(sizes, shift):
    places = list(itertools.product(*[range(n) for n in sizes]))
    return [
        (i, places.index(tuple((a + b) % n for a, b, n in zip(place, shift, sizes)))) for i, place in enumerate(places)
    ]


def wrap(i, n):
    return jnp.where(i >= n, i - n, i)


def dest(shard, j, n):
    if n & (n - 1) == 0:
        return shard ^ j
    return (shard + j) % n


def source(shard, j, n):
    if n & (n - 1) == 0:
        return shard ^ j
    return (shard + n - j) % n


def slot_groups(n):
    late = [n // 2] if n > 1 else []
    return [j for j in range(n) if j not in late], late


def start_order(n):
    return list(range(n - 1, n // 2 - 1, -1)) + list(range(1, n // 2))


def start_tables(query_hbm, pairs_hbm, query_row, pairs, sem):
    copies = [pltpu.make_async_copy(query_hbm, query_row, sem.at[0]), pltpu.make_async_copy(pairs_hbm, pairs, sem.at[1])]
    for copy in copies:
        copy.start()
    return copies


def table_scratch(query_row, pairs):
    return [pltpu.SMEM(query_row.shape, query_row.dtype), pltpu.SMEM(pairs.shape, pairs.dtype)]


def pick_rows(query_row, pairs, per_owner, dests):
    base = lax.axis_index("shard") * per_owner
    layer = lax.axis_index("layer")

    def step(q, rows):
        row = query_row[q] - base
        held = jnp.logical_and(row >= 0, row < per_owner)
        row = jnp.where(held, row, 0)
        return tuple(r + pairs[layer, to, q] * row for r, to in zip(rows, dests))

    count = query_row.shape[0]
    rows = lax.fori_loop(0, count, step, (jnp.int32(0),) * len(dests), unroll=count <= 16)
    return [jnp.clip(row, 0, per_owner - 1) for row in rows]


def span(part, wide):
    return pl.ds(pl.multiple_of(part * wide, 128), wide)


def send_kernel(parts, shard_count, query_hbm, pairs_hbm, act, grad, factor_in, factor_out, *refs):
    sent, (query_row, pairs, stored, sem, table_sem) = refs[:-5], refs[-5:]
    tables = start_tables(query_hbm, pairs_hbm, query_row, pairs, table_sem)
    my_part, my_shard = lax.axis_index("parts"), lax.axis_index("shard")
    wide_out, wide_in = grad.shape[2] // parts, act.shape[2] // parts
    to_out, to_in = pl.ds(0, wide_out), pl.ds(wide_out, wide_in)
    copies = []

    def start(piece, target):
        copies.append(pltpu.make_async_copy(piece, target, sem.at[len(copies)]))
        copies[-1].start()

    start(factor_out.at[0, :, :, span(my_part, wide_out)], stored.at[:, :, to_out])
    start(factor_in.at[0, :, :, span(my_part, wide_in)], stored.at[:, :, to_in])
    for e in range(1, parts):
        part = wrap(my_part + e, parts)
        start(grad.at[0, :, span(part, wide_out)], sent[shard_count - 1 + e - 1].at[:, to_out])
        start(act.at[0, :, span(part, wide_in)], sent[shard_count - 1 + e - 1].at[:, to_in])
    for table in tables:
        table.wait()
    dests = [dest(my_shard, j, shard_count) for j in range(1, shard_count)]
    listed = pick_rows(query_row, pairs, factor_out.shape[1], dests)
    for copy in copies[:2]:
        copy.wait()
    for target, row in zip(sent, listed):
        target[...] = stored[row]
    for copy in copies[2:]:
        copy.wait()


def make_sends(act, grad, factor_in, factor_out, query_row, pairs):
    parts, shard_count = lax.axis_size("parts"), lax.axis_size("shard")
    rank, tokens = factor_out.shape[2], act.shape[1]
    wide = (grad.shape[2] + act.shape[2]) // parts
    shapes = [pltpu.VMEM((rank, wide), act.dtype)] * (shard_count - 1)
    shapes += [pltpu.VMEM((tokens, wide), act.dtype)] * (parts - 1)
    sent = pl.pallas_call(
        functools.partial(send_kernel, parts, shard_count),
        out_shape=shapes,
        in_specs=[pl.BlockSpec(memory_space=pltpu.HBM)] * 6,
        out_specs=[pl.BlockSpec(memory_space=pltpu.VMEM)] * len(shapes),
        scratch_shapes=table_scratch(query_row, pairs)
        + [
            pltpu.VMEM((factor_out.shape[1], rank, wide), act.dtype),
            pltpu.SemaphoreType.DMA((2 * parts,)),
            pltpu.SemaphoreType.DMA((2,)),
        ],
        compiler_params=pltpu.CompilerParams(vmem_limit_bytes=2**23),
        name="make_sends",
    )(query_row, pairs, act, grad, factor_in, factor_out)
    return sent[: shard_count - 1], sent[shard_count - 1 :]


def own_kernel(parts, order, query_hbm, pairs_hbm, act, grad, factor_in, factor_out, rows, *refs):
    slots, (weights, query_row, pairs, sem, table_sem) = refs[:parts], refs[parts:]
    tables = start_tables(query_hbm, pairs_hbm, query_row, pairs, table_sem)
    my_part, my_shard, my_layer = lax.axis_index("parts"), lax.axis_index("shard"), lax.axis_index("layer")
    layers, shard_count = lax.axis_size("layer"), lax.axis_size("shard")
    per_owner, tokens = factor_out.shape[1], rows.shape[0]
    wide_out, wide_in = grad.shape[2] // parts, act.shape[2] // parts
    to_out, to_in = pl.ds(0, wide_out), pl.ds(wide_out, wide_in)
    copies = []

    def start(piece, target):
        copies.append(pltpu.make_async_copy(piece, target, sem.at[len(copies)]))
        copies[-1].start()

    start(grad.at[0, :, span(my_part, wide_out)], rows.at[:, to_out])
    start(act.at[0, :, span(my_part, wide_in)], rows.at[:, to_in])
    for table in tables:
        table.wait()
    (row,) = pick_rows(query_row, pairs, per_owner, [my_shard])
    for e, slot in enumerate(slots):
        part = wrap(my_part + e, parts)
        start(factor_out.at[0, row, :, span(part, wide_out)], slot.at[:, to_out])
        start(factor_in.at[0, row, :, span(part, wide_in)], slot.at[:, to_in])
    wide = query_row.shape[0] // layers
    for e in range(layers):
        layer = wrap(my_layer + e, layers)
        for i in range(wide):
            q = layer * wide + i
            listed = pairs[my_layer, my_shard, q]
            for k, j in enumerate(order):
                row = query_row[q] - source(my_shard, j, shard_count) * per_owner
                here = jnp.logical_and(row >= 0, row < per_owner)
                weight = jnp.where(here, listed, 0).astype(jnp.float32)
                weights[e, k, i : i + 1, :] = jnp.full((1, tokens), weight, jnp.float32)
    for copy in copies:
        copy.wait()


def make_own(order, act, grad, factor_in, factor_out, query_row, pairs):
    parts, layers = lax.axis_size("parts"), lax.axis_size("layer")
    rank, tokens = factor_out.shape[2], act.shape[1]
    wide = (grad.shape[2] + act.shape[2]) // parts
    shapes = [
        pltpu.VMEM((tokens, wide), act.dtype),
        *[pltpu.VMEM((rank, wide), act.dtype)] * parts,
        pltpu.VMEM((layers, len(order), query_row.shape[0] // layers, tokens), jnp.float32),
    ]
    return pl.pallas_call(
        functools.partial(own_kernel, parts, tuple(order)),
        out_shape=shapes,
        in_specs=[pl.BlockSpec(memory_space=pltpu.HBM)] * 6,
        out_specs=[pl.BlockSpec(memory_space=pltpu.VMEM)] * len(shapes),
        scratch_shapes=table_scratch(query_row, pairs)
        + [pltpu.SemaphoreType.DMA((2 + 2 * parts,)), pltpu.SemaphoreType.DMA((2,))],
        compiler_params=pltpu.CompilerParams(vmem_limit_bytes=2**22),
        name="make_own",
    )(query_row, pairs, act, grad, factor_in, factor_out)


def vmem_call(kernel, shapes, inputs, flops=0):
    vmem = pl.BlockSpec(memory_space=pltpu.VMEM)
    inputs = [pltpu.with_memory_space_constraint(x, pltpu.VMEM) for x in inputs]
    read = sum(x.size * x.dtype.itemsize for x in inputs)
    return pl.pallas_call(
        kernel,
        out_shape=[pltpu.VMEM(shape, jnp.float32) for shape in shapes],
        in_specs=[vmem] * len(inputs),
        out_specs=[vmem] * len(shapes),
        compiler_params=pltpu.CompilerParams(vmem_limit_bytes=2**23),
        cost_estimate=pl.CostEstimate(flops=flops, bytes_accessed=read, transcendentals=0),
    )(*inputs)


def project_kernel(slot_count, wide_out, *refs):
    slots, rows, out = refs[:slot_count], refs[slot_count], refs[-1]
    rank, wide = slots[0].shape
    for which, (low, high) in enumerate(((0, wide_out), (wide_out, wide))):
        left = jnp.concatenate([slot[:, low:high] for slot in slots], axis=0)
        proj = lax.dot_general(left, rows[:, low:high], (((1,), (1,)), ((), ())), preferred_element_type=jnp.float32)
        for j in range(slot_count):
            out[which, j] = proj[j * rank : (j + 1) * rank]


def project(slots, rows, wide_out):
    (rank, wide), tokens = slots[0].shape, rows.shape[0]
    kernel = functools.partial(project_kernel, len(slots), wide_out)
    flops = 2 * len(slots) * rank * tokens * wide
    return vmem_call(kernel, [(2, len(slots), rank, tokens)], [*slots, rows], flops)[0]


def local_kernel(wide_out, *refs):
    count = len(refs) // 2
    slots, rows, out = refs[:count], refs[count:-1], refs[-1]
    for which, (low, high) in enumerate(((0, wide_out), (wide_out, slots[0].shape[1]))):
        total = None
        for slot, block in zip(slots, rows):
            proj = lax.dot_general(
                slot[:, low:high], block[:, low:high], (((1,), (1,)), ((), ())), preferred_element_type=jnp.float32
            )
            total = proj if total is None else total + proj
        out[which, 0] = total


def project_local(slots, rows, wide_out):
    (rank, wide), tokens = slots[0].shape, rows[0].shape[0]
    kernel = functools.partial(local_kernel, wide_out)
    return vmem_call(kernel, [(2, 1, rank, tokens)], [*slots, *rows], 2 * len(slots) * rank * tokens * wide)[0]


def join_kernel(counts, *refs):
    pieces, out = list(refs[:-1]), refs[-1]
    done = 0
    for count in counts:
        group = [pieces.pop(0) for _ in range(count)]
        total = group[0][...]
        for piece in group[1:]:
            total = total + piece[...]
        out[:, done : done + total.shape[1]] = total
        done += total.shape[1]


def join(groups):
    slots = sum(group[0].shape[1] for group in groups)
    kernel = functools.partial(join_kernel, [len(group) for group in groups])
    shape = (2, slots, *groups[0][0].shape[2:])
    return vmem_call(kernel, [shape], [piece for group in groups for piece in group])[0]


def score_kernel(weights, *refs):
    layers, slots = weights.shape[:2]
    pieces, outs = refs[:-layers], refs[-layers:]
    total = pieces[0][...]
    for piece in pieces[1:]:
        total = total + piece[...]
    scores = [jnp.sum(total[0, k] * total[1, k], axis=0, keepdims=True) for k in range(slots)]
    for e, out in enumerate(outs):
        block = weights[e, 0] * scores[0]
        for k in range(1, slots):
            block = block + weights[e, k] * scores[k]
        out[...] = block


def make_scores(weights, pieces):
    layers, _, wide, tokens = weights.shape
    return vmem_call(score_kernel, [(wide, tokens)] * layers, [weights, *pieces])


def shards(act_in, grad_out, factor_in, factor_out, query_row, pairs):
    parts = lax.axis_size("parts")
    shard_count = lax.axis_size("shard")
    layers = lax.axis_size("layer")
    subs = lax.axis_size("sub")
    wide_out = grad_out.shape[2] // parts
    early, late = slot_groups(shard_count)

    args = [
        pltpu.with_memory_space_constraint(x, pltpu.HBM)
        for x in (act_in, grad_out, factor_in, factor_out, query_row, pairs)
    ]
    sent_slots, sent_rows = make_sends(*args)
    rows = []
    for e in range(1, parts):
        rows.append(lax.ppermute(sent_rows[e - 1], "parts", shifted((parts,), (e,))))
    slots = [None] * shard_count
    for j in start_order(shard_count):
        to = [(i, dest(i, j, shard_count)) for i in range(shard_count)]
        slots[j] = lax.ppermute(sent_slots[j - 1], "shard", to)
    own_rows, *own_slots, weights = make_own(early + late, *args)

    groups = [[project_local(own_slots, [own_rows] + list(sent_rows), wide_out)]]

    def sums(numbers):
        if not numbers:
            return
        group = []
        for e, block in enumerate(rows, 1):
            part_sums = project([slots[j] for j in numbers], block, wide_out)
            group.append(lax.ppermute(part_sums, "parts", shifted((parts,), (parts - e,))))
        group.insert(0, project([slots[j] for j in numbers], own_rows, wide_out))
        groups.append(group)

    sums(early[1:])
    sums(late)
    whole = [join(groups)]
    for f in range(1, subs):
        whole.append(lax.ppermute(whole[0], "sub", shifted((subs,), (f,))))
    blocks = make_scores(weights, whole)

    out = blocks[0]
    for e in range(1, layers):
        out = out + lax.ppermute(blocks[e], "layer", shifted((layers,), (e,)))
    return out.T


def solution(mesh):
    in_specs = (
        P("layer", ("parts", "shard"), "sub"),
        P("layer", ("parts", "shard"), "sub"),
        P("layer", "shard", None, "sub"),
        P("layer", "shard", None, "sub"),
        P(),
        P(),
    )
    out_specs = P(("parts", "shard"), "layer")

    return jax.shard_map(shards, mesh=mesh, in_specs=in_specs, out_specs=out_specs, check_vma=False)
```

```python
import functools
import itertools

import jax
import jax.numpy as jnp
from jax import lax
from jax.experimental import pallas as pl
from jax.experimental.pallas import tpu as pltpu
from jax.sharding import PartitionSpec as P


def shifted(sizes, shift):
    places = list(itertools.product(*[range(n) for n in sizes]))
    return [
        (i, places.index(tuple((a + b) % n for a, b, n in zip(place, shift, sizes)))) for i, place in enumerate(places)
    ]


def wrap(i, n):
    return jnp.where(i >= n, i - n, i)


def dest(shard, j, n):
    if n & (n - 1) == 0:
        return shard ^ j
    return (shard + j) % n


def source(shard, j, n):
    if n & (n - 1) == 0:
        return shard ^ j
    return (shard + n - j) % n


def slot_groups(n):
    late = [n // 2] if n > 1 else []
    return [j for j in range(n) if j not in late], late


def start_order(n):
    return list(range(n - 1, n // 2 - 1, -1)) + list(range(1, n // 2))


def start_tables(query_hbm, pairs_hbm, query_row, pairs, sem):
    copies = [pltpu.make_async_copy(query_hbm, query_row, sem.at[0]), pltpu.make_async_copy(pairs_hbm, pairs, sem.at[1])]
    for copy in copies:
        copy.start()
    return copies


def table_scratch(query_row, pairs):
    return [pltpu.SMEM(query_row.shape, query_row.dtype), pltpu.SMEM(pairs.shape, pairs.dtype)]


def pick_rows(query_row, pairs, per_owner, dests):
    base = lax.axis_index("shard") * per_owner
    layer = lax.axis_index("layer")

    def step(q, rows):
        row = query_row[q] - base
        held = jnp.logical_and(row >= 0, row < per_owner)
        row = jnp.where(held, row, 0)
        return tuple(r + pairs[layer, to, q] * row for r, to in zip(rows, dests))

    count = query_row.shape[0]
    rows = lax.fori_loop(0, count, step, (jnp.int32(0),) * len(dests), unroll=count <= 16)
    return [jnp.clip(row, 0, per_owner - 1) for row in rows]


def span(part, wide):
    return pl.ds(pl.multiple_of(part * wide, 128), wide)


def send_kernel(parts, shard_count, query_hbm, pairs_hbm, act, grad, factor_in, factor_out, *refs):
    sent, (query_row, pairs, stored, sem, table_sem) = refs[:-5], refs[-5:]
    tables = start_tables(query_hbm, pairs_hbm, query_row, pairs, table_sem)
    my_part, my_shard = lax.axis_index("parts"), lax.axis_index("shard")
    wide_out, wide_in = grad.shape[2] // parts, act.shape[2] // parts
    to_out, to_in = pl.ds(0, wide_out), pl.ds(wide_out, wide_in)
    copies = []

    def start(piece, target):
        copies.append(pltpu.make_async_copy(piece, target, sem.at[len(copies)]))
        copies[-1].start()

    start(factor_out.at[0, :, :, span(my_part, wide_out)], stored.at[:, :, to_out])
    start(factor_in.at[0, :, :, span(my_part, wide_in)], stored.at[:, :, to_in])
    for e in range(1, parts):
        part = wrap(my_part + e, parts)
        start(grad.at[0, :, span(part, wide_out)], sent[shard_count - 1 + e - 1].at[:, to_out])
        start(act.at[0, :, span(part, wide_in)], sent[shard_count - 1 + e - 1].at[:, to_in])
    for table in tables:
        table.wait()
    dests = [dest(my_shard, j, shard_count) for j in range(1, shard_count)]
    listed = pick_rows(query_row, pairs, factor_out.shape[1], dests)
    for copy in copies[:2]:
        copy.wait()
    for target, row in zip(sent, listed):
        target[...] = stored[row]
    for copy in copies[2:]:
        copy.wait()


def make_sends(act, grad, factor_in, factor_out, query_row, pairs):
    parts, shard_count = lax.axis_size("parts"), lax.axis_size("shard")
    rank, tokens = factor_out.shape[2], act.shape[1]
    wide = (grad.shape[2] + act.shape[2]) // parts
    shapes = [pltpu.VMEM((rank, wide), act.dtype)] * (shard_count - 1)
    shapes += [pltpu.VMEM((tokens, wide), act.dtype)] * (parts - 1)
    sent = pl.pallas_call(
        functools.partial(send_kernel, parts, shard_count),
        out_shape=shapes,
        in_specs=[pl.BlockSpec(memory_space=pltpu.HBM)] * 6,
        out_specs=[pl.BlockSpec(memory_space=pltpu.VMEM)] * len(shapes),
        scratch_shapes=table_scratch(query_row, pairs)
        + [
            pltpu.VMEM((factor_out.shape[1], rank, wide), act.dtype),
            pltpu.SemaphoreType.DMA((2 * parts,)),
            pltpu.SemaphoreType.DMA((2,)),
        ],
        compiler_params=pltpu.CompilerParams(vmem_limit_bytes=2**23),
        name="make_sends",
    )(query_row, pairs, act, grad, factor_in, factor_out)
    return sent[: shard_count - 1], sent[shard_count - 1 :]


def own_kernel(parts, order, query_hbm, pairs_hbm, act, grad, factor_in, factor_out, rows, *refs):
    slots, (weights, query_row, pairs, sem, table_sem) = refs[:parts], refs[parts:]
    tables = start_tables(query_hbm, pairs_hbm, query_row, pairs, table_sem)
    my_part, my_shard, my_layer = lax.axis_index("parts"), lax.axis_index("shard"), lax.axis_index("layer")
    layers, shard_count = lax.axis_size("layer"), lax.axis_size("shard")
    per_owner, tokens = factor_out.shape[1], rows.shape[0]
    wide_out, wide_in = grad.shape[2] // parts, act.shape[2] // parts
    to_out, to_in = pl.ds(0, wide_out), pl.ds(wide_out, wide_in)
    copies = []

    def start(piece, target):
        copies.append(pltpu.make_async_copy(piece, target, sem.at[len(copies)]))
        copies[-1].start()

    start(grad.at[0, :, span(my_part, wide_out)], rows.at[:, to_out])
    start(act.at[0, :, span(my_part, wide_in)], rows.at[:, to_in])
    for table in tables:
        table.wait()
    (row,) = pick_rows(query_row, pairs, per_owner, [my_shard])
    for e, slot in enumerate(slots):
        part = wrap(my_part + e, parts)
        start(factor_out.at[0, row, :, span(part, wide_out)], slot.at[:, to_out])
        start(factor_in.at[0, row, :, span(part, wide_in)], slot.at[:, to_in])
    wide = query_row.shape[0] // layers
    for e in range(layers):
        layer = wrap(my_layer + e, layers)
        for i in range(wide):
            q = layer * wide + i
            listed = pairs[my_layer, my_shard, q]
            for k, j in enumerate(order):
                row = query_row[q] - source(my_shard, j, shard_count) * per_owner
                here = jnp.logical_and(row >= 0, row < per_owner)
                weight = jnp.where(here, listed, 0).astype(jnp.float32)
                weights[e, k, i : i + 1, :] = jnp.full((1, tokens), weight, jnp.float32)
    for copy in copies:
        copy.wait()


def make_own(order, act, grad, factor_in, factor_out, query_row, pairs):
    parts, layers = lax.axis_size("parts"), lax.axis_size("layer")
    rank, tokens = factor_out.shape[2], act.shape[1]
    wide = (grad.shape[2] + act.shape[2]) // parts
    shapes = [
        pltpu.VMEM((tokens, wide), act.dtype),
        *[pltpu.VMEM((rank, wide), act.dtype)] * parts,
        pltpu.VMEM((layers, len(order), query_row.shape[0] // layers, tokens), jnp.float32),
    ]
    return pl.pallas_call(
        functools.partial(own_kernel, parts, tuple(order)),
        out_shape=shapes,
        in_specs=[pl.BlockSpec(memory_space=pltpu.HBM)] * 6,
        out_specs=[pl.BlockSpec(memory_space=pltpu.VMEM)] * len(shapes),
        scratch_shapes=table_scratch(query_row, pairs)
        + [pltpu.SemaphoreType.DMA((2 + 2 * parts,)), pltpu.SemaphoreType.DMA((2,))],
        compiler_params=pltpu.CompilerParams(vmem_limit_bytes=2**22),
        name="make_own",
    )(query_row, pairs, act, grad, factor_in, factor_out)


def vmem_call(kernel, shapes, inputs, flops=0):
    vmem = pl.BlockSpec(memory_space=pltpu.VMEM)
    inputs = [pltpu.with_memory_space_constraint(x, pltpu.VMEM) for x in inputs]
    read = sum(x.size * x.dtype.itemsize for x in inputs)
    return pl.pallas_call(
        kernel,
        out_shape=[pltpu.VMEM(shape, jnp.float32) for shape in shapes],
        in_specs=[vmem] * len(inputs),
        out_specs=[vmem] * len(shapes),
        compiler_params=pltpu.CompilerParams(vmem_limit_bytes=2**23),
        cost_estimate=pl.CostEstimate(flops=flops, bytes_accessed=read, transcendentals=0),
    )(*inputs)


def project_kernel(slot_count, wide_out, *refs):
    slots, rows, out = refs[:slot_count], refs[slot_count], refs[-1]
    rank, wide = slots[0].shape
    for which, (low, high) in enumerate(((0, wide_out), (wide_out, wide))):
        left = jnp.concatenate([slot[:, low:high] for slot in slots], axis=0)
        proj = lax.dot_general(left, rows[:, low:high], (((1,), (1,)), ((), ())), preferred_element_type=jnp.float32)
        for j in range(slot_count):
            out[which, j] = proj[j * rank : (j + 1) * rank]


def project(slots, rows, wide_out):
    (rank, wide), tokens = slots[0].shape, rows.shape[0]
    kernel = functools.partial(project_kernel, len(slots), wide_out)
    flops = 2 * len(slots) * rank * tokens * wide
    return vmem_call(kernel, [(2, len(slots), rank, tokens)], [*slots, rows], flops)[0]


def local_kernel(wide_out, *refs):
    count = len(refs) // 2
    slots, rows, out = refs[:count], refs[count:-1], refs[-1]
    for which, (low, high) in enumerate(((0, wide_out), (wide_out, slots[0].shape[1]))):
        total = None
        for slot, block in zip(slots, rows):
            proj = lax.dot_general(
                slot[:, low:high], block[:, low:high], (((1,), (1,)), ((), ())), preferred_element_type=jnp.float32
            )
            total = proj if total is None else total + proj
        out[which, 0] = total


def project_local(slots, rows, wide_out):
    (rank, wide), tokens = slots[0].shape, rows[0].shape[0]
    kernel = functools.partial(local_kernel, wide_out)
    return vmem_call(kernel, [(2, 1, rank, tokens)], [*slots, *rows], 2 * len(slots) * rank * tokens * wide)[0]


def join_kernel(counts, *refs):
    pieces, out = list(refs[:-1]), refs[-1]
    done = 0
    for count in counts:
        group = [pieces.pop(0) for _ in range(count)]
        total = group[0][...]
        for piece in group[1:]:
            total = total + piece[...]
        out[:, done : done + total.shape[1]] = total
        done += total.shape[1]


def join(groups):
    slots = sum(group[0].shape[1] for group in groups)
    kernel = functools.partial(join_kernel, [len(group) for group in groups])
    shape = (2, slots, *groups[0][0].shape[2:])
    return vmem_call(kernel, [shape], [piece for group in groups for piece in group])[0]


def score_kernel(whole_count, weights, *refs):
    layers, slots = weights.shape[:2]
    pieces, outs = refs[:-layers], refs[-layers:]

    def add(refs):
        total = refs[0][...]
        for ref in refs[1:]:
            total = total + ref[...]
        return total

    total, parted = add(pieces[:whole_count]), pieces[whole_count:]
    scores = []
    if parted:
        last = add(parted)
        first = slots - last.shape[1]
        last = total[:, first:] + last
        scores = [jnp.sum(last[0, k] * last[1, k], axis=0, keepdims=True) for k in range(slots - first)]
    scores = [jnp.sum(total[0, k] * total[1, k], axis=0, keepdims=True) for k in range(slots - len(scores))] + scores
    for e, out in enumerate(outs):
        block = weights[e, 0] * scores[0]
        for k in range(1, slots):
            block = block + weights[e, k] * scores[k]
        out[...] = block


def make_scores(weights, whole, parted):
    layers, _, wide, tokens = weights.shape
    kernel = functools.partial(score_kernel, len(whole))
    return vmem_call(kernel, [(wide, tokens)] * layers, [weights, *whole, *parted])


def shards(act_in, grad_out, factor_in, factor_out, query_row, pairs):
    parts = lax.axis_size("parts")
    shard_count = lax.axis_size("shard")
    layers = lax.axis_size("layer")
    subs = lax.axis_size("sub")
    wide_out = grad_out.shape[2] // parts
    early, late = slot_groups(shard_count)

    args = [
        pltpu.with_memory_space_constraint(x, pltpu.HBM)
        for x in (act_in, grad_out, factor_in, factor_out, query_row, pairs)
    ]
    sent_slots, sent_rows = make_sends(*args)
    rows = []
    for e in range(1, parts):
        rows.append(lax.ppermute(sent_rows[e - 1], "parts", shifted((parts,), (e,))))
    slots = [None] * shard_count
    for j in start_order(shard_count):
        to = [(i, dest(i, j, shard_count)) for i in range(shard_count)]
        slots[j] = lax.ppermute(sent_slots[j - 1], "shard", to)
    own_rows, *own_slots, weights = make_own(early + late, *args)

    groups = [[project_local(own_slots, [own_rows] + list(sent_rows), wide_out)]]
    early_group, late_group, late_got = [], [], []
    for e, block in enumerate(rows, 1):
        part_sums = project([slots[j] for j in early[1:]], block, wide_out)
        early_group.append(lax.ppermute(part_sums, "parts", shifted((parts,), (parts - e,))))
        part_sums = project([slots[j] for j in late], block, wide_out)
        for f in range(subs):
            late_got.append(lax.ppermute(part_sums, ("parts", "sub"), shifted((parts, subs), (parts - e, f))))
    early_group.insert(0, project([slots[j] for j in early[1:]], own_rows, wide_out))
    late_group.append(project([slots[j] for j in late], own_rows, wide_out))
    whole = [join([*groups, early_group, late_group])]
    for f in range(1, subs):
        whole.append(lax.ppermute(whole[0], "sub", shifted((subs,), (f,))))
    blocks = make_scores(weights, whole, late_got)

    out = blocks[0]
    for e in range(1, layers):
        out = out + lax.ppermute(blocks[e], "layer", shifted((layers,), (e,)))
    return out.T


def solution(mesh):
    in_specs = (
        P("layer", ("parts", "shard"), "sub"),
        P("layer", ("parts", "shard"), "sub"),
        P("layer", "shard", None, "sub"),
        P("layer", "shard", None, "sub"),
        P(),
        P(),
    )
    out_specs = P(("parts", "shard"), "layer")

    return jax.shard_map(shards, mesh=mesh, in_specs=in_specs, out_specs=out_specs, check_vma=False)
```

```python
import functools
import itertools

import jax
import jax.numpy as jnp
from jax import lax
from jax.experimental import pallas as pl
from jax.experimental.pallas import tpu as pltpu
from jax.sharding import PartitionSpec as P


def shifted(sizes, shift):
    places = list(itertools.product(*[range(n) for n in sizes]))
    return [
        (i, places.index(tuple((a + b) % n for a, b, n in zip(place, shift, sizes)))) for i, place in enumerate(places)
    ]


def wrap(i, n):
    return jnp.where(i >= n, i - n, i)


def dest(shard, j, n):
    if n & (n - 1) == 0:
        return shard ^ j
    return (shard + j) % n


def source(shard, j, n):
    if n & (n - 1) == 0:
        return shard ^ j
    return (shard + n - j) % n


def slot_groups(n):
    late = [n - 1] if n > 1 else []
    return [j for j in range(n) if j not in late], late


def start_order(n):
    return list(range(max(1, n // 2), n)) + list(range(1, n // 2))


def start_tables(query_hbm, pairs_hbm, query_row, pairs, sem):
    copies = [pltpu.make_async_copy(query_hbm, query_row, sem.at[0]), pltpu.make_async_copy(pairs_hbm, pairs, sem.at[1])]
    for copy in copies:
        copy.start()
    return copies


def table_scratch(query_row, pairs):
    return [pltpu.SMEM(query_row.shape, query_row.dtype), pltpu.SMEM(pairs.shape, pairs.dtype)]


def pick_rows(query_row, pairs, per_owner, dests):
    base = lax.axis_index("shard") * per_owner
    layer = lax.axis_index("layer")

    def step(q, rows):
        row = query_row[q] - base
        held = jnp.logical_and(row >= 0, row < per_owner)
        row = jnp.where(held, row, 0)
        return tuple(r + pairs[layer, to, q] * row for r, to in zip(rows, dests))

    count = query_row.shape[0]
    rows = lax.fori_loop(0, count, step, (jnp.int32(0),) * len(dests), unroll=count <= 16)
    return [jnp.clip(row, 0, per_owner - 1) for row in rows]


def span(part, wide):
    return pl.ds(pl.multiple_of(part * wide, 128), wide)


def send_kernel(parts, shard_count, query_hbm, pairs_hbm, act, grad, factor_in, factor_out, *refs):
    sent, (query_row, pairs, stored, sem, table_sem) = refs[:-5], refs[-5:]
    tables = start_tables(query_hbm, pairs_hbm, query_row, pairs, table_sem)
    my_part, my_shard = lax.axis_index("parts"), lax.axis_index("shard")
    wide_out, wide_in = grad.shape[2] // parts, act.shape[2] // parts
    to_out, to_in = pl.ds(0, wide_out), pl.ds(wide_out, wide_in)
    copies = []

    def start(piece, target):
        copies.append(pltpu.make_async_copy(piece, target, sem.at[len(copies)]))
        copies[-1].start()

    start(factor_out.at[0, :, :, span(my_part, wide_out)], stored.at[:, :, to_out])
    start(factor_in.at[0, :, :, span(my_part, wide_in)], stored.at[:, :, to_in])
    for e in range(1, parts):
        part = wrap(my_part + e, parts)
        start(grad.at[0, :, span(part, wide_out)], sent[shard_count - 1 + e - 1].at[:, to_out])
        start(act.at[0, :, span(part, wide_in)], sent[shard_count - 1 + e - 1].at[:, to_in])
    for table in tables:
        table.wait()
    dests = [dest(my_shard, j, shard_count) for j in range(1, shard_count)]
    listed = pick_rows(query_row, pairs, factor_out.shape[1], dests)
    for copy in copies[:2]:
        copy.wait()
    for target, row in zip(sent, listed):
        target[...] = stored[row]
    for copy in copies[2:]:
        copy.wait()


def make_sends(act, grad, factor_in, factor_out, query_row, pairs):
    parts, shard_count = lax.axis_size("parts"), lax.axis_size("shard")
    rank, tokens = factor_out.shape[2], act.shape[1]
    wide = (grad.shape[2] + act.shape[2]) // parts
    shapes = [pltpu.VMEM((rank, wide), act.dtype)] * (shard_count - 1)
    shapes += [pltpu.VMEM((tokens, wide), act.dtype)] * (parts - 1)
    sent = pl.pallas_call(
        functools.partial(send_kernel, parts, shard_count),
        out_shape=shapes,
        in_specs=[pl.BlockSpec(memory_space=pltpu.HBM)] * 6,
        out_specs=[pl.BlockSpec(memory_space=pltpu.VMEM)] * len(shapes),
        scratch_shapes=table_scratch(query_row, pairs)
        + [
            pltpu.VMEM((factor_out.shape[1], rank, wide), act.dtype),
            pltpu.SemaphoreType.DMA((2 * parts,)),
            pltpu.SemaphoreType.DMA((2,)),
        ],
        compiler_params=pltpu.CompilerParams(vmem_limit_bytes=2**23),
        name="make_sends",
    )(query_row, pairs, act, grad, factor_in, factor_out)
    return sent[: shard_count - 1], sent[shard_count - 1 :]


def own_kernel(parts, order, query_hbm, pairs_hbm, act, grad, factor_in, factor_out, rows, *refs):
    slots, (weights, query_row, pairs, sem, table_sem) = refs[:parts], refs[parts:]
    tables = start_tables(query_hbm, pairs_hbm, query_row, pairs, table_sem)
    my_part, my_shard, my_layer = lax.axis_index("parts"), lax.axis_index("shard"), lax.axis_index("layer")
    layers, shard_count = lax.axis_size("layer"), lax.axis_size("shard")
    per_owner, tokens = factor_out.shape[1], rows.shape[0]
    wide_out, wide_in = grad.shape[2] // parts, act.shape[2] // parts
    to_out, to_in = pl.ds(0, wide_out), pl.ds(wide_out, wide_in)
    copies = []

    def start(piece, target):
        copies.append(pltpu.make_async_copy(piece, target, sem.at[len(copies)]))
        copies[-1].start()

    start(grad.at[0, :, span(my_part, wide_out)], rows.at[:, to_out])
    start(act.at[0, :, span(my_part, wide_in)], rows.at[:, to_in])
    for table in tables:
        table.wait()
    (row,) = pick_rows(query_row, pairs, per_owner, [my_shard])
    for e, slot in enumerate(slots):
        part = wrap(my_part + e, parts)
        start(factor_out.at[0, row, :, span(part, wide_out)], slot.at[:, to_out])
        start(factor_in.at[0, row, :, span(part, wide_in)], slot.at[:, to_in])
    wide = query_row.shape[0] // layers
    for e in range(layers):
        layer = wrap(my_layer + e, layers)
        for i in range(wide):
            q = layer * wide + i
            listed = pairs[my_layer, my_shard, q]
            for k, j in enumerate(order):
                row = query_row[q] - source(my_shard, j, shard_count) * per_owner
                here = jnp.logical_and(row >= 0, row < per_owner)
                weight = jnp.where(here, listed, 0).astype(jnp.float32)
                weights[e, k, i : i + 1, :] = jnp.full((1, tokens), weight, jnp.float32)
    for copy in copies:
        copy.wait()


def make_own(order, act, grad, factor_in, factor_out, query_row, pairs):
    parts, layers = lax.axis_size("parts"), lax.axis_size("layer")
    rank, tokens = factor_out.shape[2], act.shape[1]
    wide = (grad.shape[2] + act.shape[2]) // parts
    shapes = [
        pltpu.VMEM((tokens, wide), act.dtype),
        *[pltpu.VMEM((rank, wide), act.dtype)] * parts,
        pltpu.VMEM((layers, len(order), query_row.shape[0] // layers, tokens), jnp.float32),
    ]
    return pl.pallas_call(
        functools.partial(own_kernel, parts, tuple(order)),
        out_shape=shapes,
        in_specs=[pl.BlockSpec(memory_space=pltpu.HBM)] * 6,
        out_specs=[pl.BlockSpec(memory_space=pltpu.VMEM)] * len(shapes),
        scratch_shapes=table_scratch(query_row, pairs)
        + [pltpu.SemaphoreType.DMA((2 + 2 * parts,)), pltpu.SemaphoreType.DMA((2,))],
        compiler_params=pltpu.CompilerParams(vmem_limit_bytes=2**22),
        name="make_own",
    )(query_row, pairs, act, grad, factor_in, factor_out)


def vmem_call(kernel, shapes, inputs, flops=0):
    vmem = pl.BlockSpec(memory_space=pltpu.VMEM)
    inputs = [pltpu.with_memory_space_constraint(x, pltpu.VMEM) for x in inputs]
    read = sum(x.size * x.dtype.itemsize for x in inputs)
    return pl.pallas_call(
        kernel,
        out_shape=[pltpu.VMEM(shape, jnp.float32) for shape in shapes],
        in_specs=[vmem] * len(inputs),
        out_specs=[vmem] * len(shapes),
        compiler_params=pltpu.CompilerParams(vmem_limit_bytes=2**23),
        cost_estimate=pl.CostEstimate(flops=flops, bytes_accessed=read, transcendentals=0),
    )(*inputs)


def project_kernel(slot_count, wide_out, *refs):
    slots, rows, out = refs[:slot_count], refs[slot_count], refs[-1]
    rank, wide = slots[0].shape
    for which, (low, high) in enumerate(((0, wide_out), (wide_out, wide))):
        left = jnp.concatenate([slot[:, low:high] for slot in slots], axis=0)
        proj = lax.dot_general(left, rows[:, low:high], (((1,), (1,)), ((), ())), preferred_element_type=jnp.float32)
        for j in range(slot_count):
            out[which, j] = proj[j * rank : (j + 1) * rank]


def project(slots, rows, wide_out):
    (rank, wide), tokens = slots[0].shape, rows.shape[0]
    kernel = functools.partial(project_kernel, len(slots), wide_out)
    flops = 2 * len(slots) * rank * tokens * wide
    return vmem_call(kernel, [(2, len(slots), rank, tokens)], [*slots, rows], flops)[0]


def local_kernel(wide_out, *refs):
    count = len(refs) // 2
    slots, rows, out = refs[:count], refs[count:-1], refs[-1]
    for which, (low, high) in enumerate(((0, wide_out), (wide_out, slots[0].shape[1]))):
        total = None
        for slot, block in zip(slots, rows):
            proj = lax.dot_general(
                slot[:, low:high], block[:, low:high], (((1,), (1,)), ((), ())), preferred_element_type=jnp.float32
            )
            total = proj if total is None else total + proj
        out[which, 0] = total


def project_local(slots, rows, wide_out):
    (rank, wide), tokens = slots[0].shape, rows[0].shape[0]
    kernel = functools.partial(local_kernel, wide_out)
    return vmem_call(kernel, [(2, 1, rank, tokens)], [*slots, *rows], 2 * len(slots) * rank * tokens * wide)[0]


def join_kernel(counts, *refs):
    pieces, out = list(refs[:-1]), refs[-1]
    done = 0
    for count in counts:
        group = [pieces.pop(0) for _ in range(count)]
        total = group[0][...]
        for piece in group[1:]:
            total = total + piece[...]
        out[:, done : done + total.shape[1]] = total
        done += total.shape[1]


def join(groups):
    slots = sum(group[0].shape[1] for group in groups)
    kernel = functools.partial(join_kernel, [len(group) for group in groups])
    shape = (2, slots, *groups[0][0].shape[2:])
    return vmem_call(kernel, [shape], [piece for group in groups for piece in group])[0]


def score_kernel(whole_count, weights, *refs):
    layers, slots = weights.shape[:2]
    pieces, outs = refs[:-layers], refs[-layers:]

    def add(refs):
        total = refs[0][...]
        for ref in refs[1:]:
            total = total + ref[...]
        return total

    total, parted = add(pieces[:whole_count]), pieces[whole_count:]
    scores = []
    if parted:
        last = add(parted)
        first = slots - last.shape[1]
        last = total[:, first:] + last
        scores = [jnp.sum(last[0, k] * last[1, k], axis=0, keepdims=True) for k in range(slots - first)]
    scores = [jnp.sum(total[0, k] * total[1, k], axis=0, keepdims=True) for k in range(slots - len(scores))] + scores
    for e, out in enumerate(outs):
        block = weights[e, 0] * scores[0]
        for k in range(1, slots):
            block = block + weights[e, k] * scores[k]
        out[...] = block


def make_scores(weights, whole, parted):
    layers, _, wide, tokens = weights.shape
    kernel = functools.partial(score_kernel, len(whole))
    return vmem_call(kernel, [(wide, tokens)] * layers, [weights, *whole, *parted])


def shards(act_in, grad_out, factor_in, factor_out, query_row, pairs):
    parts = lax.axis_size("parts")
    shard_count = lax.axis_size("shard")
    layers = lax.axis_size("layer")
    subs = lax.axis_size("sub")
    wide_out = grad_out.shape[2] // parts
    early, late = slot_groups(shard_count)

    args = [
        pltpu.with_memory_space_constraint(x, pltpu.HBM)
        for x in (act_in, grad_out, factor_in, factor_out, query_row, pairs)
    ]
    sent_slots, sent_rows = make_sends(*args)
    rows = []
    for e in range(1, parts):
        rows.append(lax.ppermute(sent_rows[e - 1], "parts", shifted((parts,), (e,))))
    slots = [None] * shard_count
    for j in start_order(shard_count):
        to = [(i, dest(i, j, shard_count)) for i in range(shard_count)]
        slots[j] = lax.ppermute(sent_slots[j - 1], "shard", to)
    own_rows, *own_slots, weights = make_own(early + late, *args)

    groups = [[project_local(own_slots, [own_rows] + list(sent_rows), wide_out)]]
    early_group, late_group, late_got = [], [], []
    for e, block in enumerate(rows, 1):
        part_sums = project([slots[j] for j in early[1:]], block, wide_out)
        to = shifted((parts, subs), (parts - e, 1 % subs))
        early_group.append(lax.ppermute(part_sums, ("parts", "sub"), to))
        part_sums = project([slots[j] for j in late], block, wide_out)
        for f in range(subs):
            late_got.append(lax.ppermute(part_sums, ("parts", "sub"), shifted((parts, subs), (parts - e, f))))
    early_group.insert(0, project([slots[j] for j in early[1:]], own_rows, wide_out))
    late_group.append(project([slots[j] for j in late], own_rows, wide_out))
    whole = [join([*groups, early_group, late_group])]
    for f in range(1, subs):
        whole.append(lax.ppermute(whole[0], "sub", shifted((subs,), (f,))))
    blocks = make_scores(weights, whole, late_got)

    out = blocks[0]
    for e in range(1, layers):
        out = out + lax.ppermute(blocks[e], "layer", shifted((layers,), (e,)))
    return out.T


def solution(mesh):
    in_specs = (
        P("layer", ("parts", "shard"), "sub"),
        P("layer", ("parts", "shard"), "sub"),
        P("layer", "shard", None, "sub"),
        P("layer", "shard", None, "sub"),
        P(),
        P(),
    )
    out_specs = P(("parts", "shard"), "layer")

    return jax.shard_map(shards, mesh=mesh, in_specs=in_specs, out_specs=out_specs, check_vma=False)
```
